32 devices in a mesh: band: 4 (over y, x), img: 8 (over z, core).
Axes of the slice: x: 2, y: 2, z: 4, core: 2. Of those that a mesh axis runs over, the one named last changes fastest.
Arguments:
- images: bfloat16 [4, 128, 3328], P('band', 'img'), may hold values from -12 to 12
- references: bfloat16 [4, 32, 3328], P('band', 'img'), may hold values from -0.08 to 0.08
- noise_weight: float32 [4, 1664], P('band'), may hold values from 0.5 to 4
- masks: int32 [4, 16, 8, 49], P('band', 'img'), may hold values from 0 to 1, as said below
Outputs:
- weighted_sums: float32 [4, 32, 3328], P('band', 'img')
- weight_totals: float32 [32], P('img')
The draws below stay inside these ranges and needn't reach their ends.
Inputs may be any that keep to these rules, and one draw needn't show every extreme that they name: `masks`: each entry is 0 or 1; translation number 49 // 2 is kept in every band, image block and orientation block.
All inputs are finite; a program needn't handle non-finite values.
Results may differ from the reference program's by a relative error of at most 0.0065.
Values may be sent and summed in bfloat16 or wider, within the bound.
No kernel may reach another device: no remote copies, remote signals or barrier semaphores. Data moves between devices by JAX's collectives and lax.ppermute only.
A program may use at most 64 MiB of HBM per device.

```python
import math
import jax
import jax.numpy as jnp
from jax import lax

COEF = 1664
BOX = 256
SIDE = 7
IMG_BLOCK = 8
ORIENT_DEV = 4
SHIFTS = 49
BANDS = 4
IMAGES = 128
ORIENT = 32
IBLOCKS = 16
OWNERS = 8


def draw_both(key):
    base = jax.random.fold_in(key, 11)
    key_refs = jax.random.fold_in(base, 0)
    key_amplitude = jax.random.fold_in(base, 1)
    key_images = jax.random.fold_in(base, 2)
    key_common = jax.random.fold_in(base, 5)
    amplitude = jnp.exp(jax.random.uniform(key_amplitude, (1, ORIENT, 1), jnp.float32, math.log(0.6), math.log(1.6)))
    projections = jax.random.normal(key_refs, (BANDS, ORIENT, 2 * COEF), jnp.float32) * 0.009 * amplitude
    common = 0.4 * jax.random.normal(key_common, (BANDS, 1, 2 * COEF), jnp.float32)
    noise = 0.67 * jax.random.normal(key_images, (BANDS, IMAGES, 2 * COEF), jnp.float32)
    pictures = noise + common
    return (jnp.clip(pictures, -12.0, 12.0), jnp.clip(projections, -0.08, 0.08))


def draw_images(key, part):
    pictures, projections = draw_both(key)
    return pictures.astype(jnp.bfloat16)


def draw_references(key, part):
    pictures, projections = draw_both(key)
    return projections.astype(jnp.bfloat16)


def draw_masks(key, part):
    key_level, key_roll = jax.random.split(jax.random.fold_in(key, 23))
    shape = (BANDS, IBLOCKS, OWNERS, SHIFTS)
    level = jax.random.randint(key_level, (1, IBLOCKS, 1, 1), 30, 96)
    roll = jax.random.randint(key_roll, shape, 0, 100)
    keep = (roll < level).astype(jnp.int32)
    center = (jnp.arange(SHIFTS, dtype=jnp.int32) == SHIFTS // 2).astype(jnp.int32)
    return jnp.maximum(keep, center[None, None, None, :])


def shard_levels(key, shape, shards, low, largest):
    def one(dim, parts):
        draws = jax.random.uniform(jax.random.fold_in(jax.random.fold_in(key, 6), dim), (parts,), jnp.float32, low / len(shards), largest / len(shards))
        return jnp.repeat(jnp.exp(draws), shape[dim] // parts).reshape((-1,) + (1,) * (len(shape) - dim - 1))

    factor_of = one(*shards[0])
    for cut in shards[1:]:
        factor_of = factor_of * one(*cut)
    return factor_of


def setup_inputs(seed: int = 0) -> dict:
    keys = jax.random.split(jax.random.key(seed), 5)
    images = draw_images(jax.random.fold_in(keys[4], 71), 0)
    references = draw_references(jax.random.fold_in(keys[4], 71), 0)
    noise_weight = jnp.clip(jnp.exp(math.log(4.0) - 2.0794415 * jax.random.uniform(keys[2], (BANDS, COEF), jnp.float32) ** shard_levels(keys[2], (BANDS, COEF), ((0, 4),), -0.2, 0.2)), 0.5, 4.0)
    masks = draw_masks(jax.random.fold_in(keys[4], 71), 0)
    return dict(images=images, references=references, noise_weight=noise_weight, masks=masks)


PENALTY = 10000.0


def shift_angles(band, coef):
    index = jnp.arange(coef, dtype=jnp.int32)
    freq_x = (index * 37 + band * 11) % 257 - 128
    freq_y = (index * 61 + band * 29) % 129
    shift_ids = jnp.arange(SIDE * SIDE, dtype=jnp.int32)
    move_x = shift_ids // SIDE - SIDE // 2
    move_y = shift_ids % SIDE - SIDE // 2
    phase = (move_x[:, None] * freq_x[None, :] + move_y[:, None] * freq_y[None, :]).astype(jnp.float32)
    angle = phase * (2.0 * math.pi / BOX)
    return jnp.cos(angle), jnp.sin(angle)


def align(pictures, cosine, sine):
    coef = cosine.shape[1]
    real = pictures[:, :coef].astype(jnp.float32)[:, None, :]
    imag = pictures[:, coef:].astype(jnp.float32)[:, None, :]
    out_real = real * cosine[None] - imag * sine[None]
    out_imag = real * sine[None] + imag * cosine[None]
    joined = jnp.concatenate([out_real, out_imag], axis=2).astype(jnp.bfloat16)
    return joined.reshape(pictures.shape[0] * cosine.shape[0], 2 * coef)


def prepare(projections, weight):
    doubled = jnp.concatenate([weight, weight])
    values = projections.astype(jnp.float32)
    weighted = (values * doubled[None, :]).astype(jnp.bfloat16)
    norms = jnp.sum(values * values * doubled[None, :], axis=1)
    return weighted, norms


def penalty(mask_block, img_block, orient_dev):
    blocks, owners, shift_count = mask_block.shape
    dropped = PENALTY * (1 - mask_block).astype(jnp.float32)
    dropped = jnp.transpose(dropped, (0, 2, 1))
    dropped = jnp.broadcast_to(dropped[:, None, :, :, None], (blocks, img_block, shift_count, owners, orient_dev))
    return dropped.reshape(blocks * img_block * shift_count, owners * orient_dev)


def band_term(aligned, weighted, norms, dropped):
    cross = lax.dot_general(aligned, weighted, (((1,), (1,)), ((), ())), preferred_element_type=jnp.float32)
    return cross - 0.5 * norms[None, :] - dropped


def posterior(total, count):
    grid = total.reshape(count, -1)
    peak = jnp.max(grid, axis=1, keepdims=True)
    raised = jnp.exp(grid - peak)
    return (raised / jnp.sum(raised, axis=1, keepdims=True)).reshape(total.shape)


def reference(images, references, noise_weight, masks):
    bands = images.shape[0]
    coef = noise_weight.shape[1]
    tables = [shift_angles(number, coef) for number in range(bands)]
    prepared = [prepare(references[number], noise_weight[number]) for number in range(bands)]
    blocks = images.shape[1] // IMG_BLOCK

    def one_block(carry, index):
        sums, totals = carry
        first = (index * IMG_BLOCK).astype(jnp.int32)
        kept = []
        score = jnp.zeros((IMG_BLOCK * SIDE * SIDE, ORIENT), jnp.float32)
        for number in range(bands):
            pictures = lax.dynamic_slice_in_dim(images[number], first, IMG_BLOCK, 0)
            current = align(pictures, tables[number][0], tables[number][1])
            mask_rows = lax.dynamic_slice_in_dim(masks[number], index.astype(jnp.int32), 1, 0)
            dropped = penalty(mask_rows, IMG_BLOCK, ORIENT_DEV)
            score = score + band_term(current, prepared[number][0], prepared[number][1], dropped)
            kept.append(current)
        prob = posterior(score, IMG_BLOCK)
        post = prob.astype(jnp.bfloat16)
        updated = []
        for number in range(bands):
            added = lax.dot_general(post, kept[number], (((0,), (0,)), ((), ())), preferred_element_type=jnp.float32)
            updated.append(sums[number] + added)
        totals = totals + jnp.sum(prob, axis=0)
        return (jnp.stack(updated), totals), None

    start_sums = jnp.zeros((bands, ORIENT, 2 * coef), jnp.float32)
    start_totals = jnp.zeros((ORIENT,), jnp.float32)
    (sums, totals), _ = lax.scan(one_block, (start_sums, start_totals), jnp.arange(blocks, dtype=jnp.int32))
    return sums, totals
```

```python
import functools
import math

import jax
import jax.numpy as jnp
from jax import lax
from jax.experimental import pallas as pl
from jax.experimental.pallas import tpu as pltpu
from jax.sharding import PartitionSpec as P

BOX = 256
PENALTY = 10000.0
LANES = 128
NEG = -3.0e38


F32 = jnp.float32
BF16 = jnp.bfloat16


def round_up(value, step):
    return -(-value // step) * step


def dot(a, b, dims):
    return lax.dot_general(a, b, (dims, ((), ())), preferred_element_type=F32)


def prepare_kernel(side, pair, slots, owned, axes, own, other, own_mask, other_mask, rotated, cosine, sine, dropped):
    half = side // 2
    coef = cosine.shape[1]
    band = lax.axis_index(axes[0])
    place = lax.axis_index(axes[1])

    shape = (8, coef)
    row = lax.broadcasted_iota(jnp.int32, shape, 0)
    index = lax.broadcasted_iota(jnp.int32, shape, 1)

    def modulo(value, period):
        count = jnp.floor((value.astype(F32) + 0.5) * (1.0 / period)).astype(jnp.int32)
        return value - count * period

    freq_x = modulo(index * 37 + band * 11, 257) - 128
    freq_y = modulo(index * 61 + band * 29, 129)
    phase = jnp.where(row < half, (row + 1) * freq_x, (row - half + 1) * freq_y)
    phase = jnp.bitwise_and(phase + BOX // 2, BOX - 1) - BOX // 2
    angle = phase.astype(F32) * (2.0 * math.pi / BOX)
    cosine[...] = jnp.cos(angle)
    sine[...] = jnp.sin(angle)

    count = own.shape[0]
    total = pair * count
    for part, source in enumerate((own, other)[:pair]):
        for start in range(0, coef, LANES):
            lanes, far = pl.ds(start, LANES), pl.ds(coef + start, LANES)

            def put(step, real, imag):
                rows = pl.ds((step + half) * total + part * count, count)
                rotated[rows, lanes] = real.astype(BF16)
                rotated[rows, far] = imag.astype(BF16)

            rotated[pl.ds(half * total + part * count, count), lanes] = source[:, lanes]
            rotated[pl.ds(half * total + part * count, count), far] = source[:, far]
            real = source[:, lanes].astype(F32)
            imag = source[:, far].astype(F32)
            for step in range(1, half + 1):
                c = cosine[step - 1 : step, lanes]
                s = sine[step - 1 : step, lanes]
                rc, rs, ic, iss = real * c, real * s, imag * c, imag * s
                put(step, rc - iss, rs + ic)
                put(-step, rc + iss, ic - rs)

    blocks, owners, shifts = own_mask.shape
    orient = slots * owned
    wide = dropped.shape[1]
    kept = own_mask[...].reshape(blocks * owners, shifts)
    if pair > 1:
        kept = jnp.concatenate([kept, other_mask[...].reshape(blocks * owners, shifts)], axis=0)
    gone = (1 - kept).astype(F32).astype(BF16)
    rows = kept.shape[0]
    column = lax.broadcasted_iota(jnp.int32, (shifts, wide), 1)
    shift = lax.broadcasted_iota(jnp.int32, (shifts, wide), 0)
    move_y = column // orient
    column_r = lax.broadcasted_iota(jnp.int32, (rows, wide), 1)
    row_r = lax.broadcasted_iota(jnp.int32, (rows, wide), 0)
    slot = (column_r % orient) // owned
    owner = jnp.bitwise_xor(slot, place // pair) * pair + place % pair
    mine = (row_r % owners == owner) & (column_r < side * orient)
    per_block = count // blocks
    spread = (
        lax.broadcasted_iota(jnp.int32, (total, rows), 0) // per_block
        == lax.broadcasted_iota(jnp.int32, (total, rows), 1) // owners
    )
    spread = spread.astype(F32).astype(BF16)
    for step in range(side):
        pick = ((shift == step * side + move_y) & (move_y < side)).astype(F32).astype(BF16)
        chosen = jnp.where(mine, dot(gone, pick, ((1,), (0,))), 0.0).astype(BF16)
        dropped[pl.ds(step * total, total), :] = PENALTY * dot(spread, chosen, ((1,), (0,)))


def score_kernel(side, slots, weight, rotated, cosine, sine, dropped, *rest):
    blocks, (partial, stacked, turned) = rest[:slots], rest[slots:]
    half = side // 2
    coef = cosine.shape[1]
    owned = blocks[0].shape[0]
    orient = slots * owned
    wide = partial.shape[1]
    for slot in range(slots):
        stacked[pl.ds(slot * owned, owned), :] = blocks[slot][...].astype(F32)
    if wide > side * orient:
        rest_rows = pl.ds(side * orient, wide - side * orient)
        turned[rest_rows, :] = jnp.zeros((wide - side * orient, 2 * coef), BF16)
    norms = jnp.zeros((orient, LANES), F32)
    for start in range(0, coef, LANES):
        lanes, far = pl.ds(start, LANES), pl.ds(coef + start, LANES)
        scale = weight[:, lanes]
        real, imag = stacked[:, lanes], stacked[:, far]
        norms = norms + (real * real + imag * imag) * scale
        real = (real * scale).astype(BF16)
        imag = (imag * scale).astype(BF16)

        def put(step, a, b):
            rows = pl.ds((step + half) * orient, orient)
            turned[rows, lanes] = a.astype(BF16)
            turned[rows, far] = b.astype(BF16)

        put(0, real, imag)
        real, imag = real.astype(F32), imag.astype(F32)
        for step in range(1, half + 1):
            c = cosine[half + step - 1 : half + step, lanes]
            s = sine[half + step - 1 : half + step, lanes]
            rc, rs, ic, iss = real * c, real * s, imag * c, imag * s
            put(step, rc + iss, ic - rs)
            put(-step, rc - iss, ic + rs)
    norms = jnp.sum(norms, axis=1, keepdims=True)
    column = lax.broadcasted_iota(jnp.int32, (orient, wide), 1)
    row = lax.broadcasted_iota(jnp.int32, (orient, wide), 0)
    same = (column % orient == row) & (column < side * orient)
    level = jnp.sum(jnp.where(same, norms, 0.0), axis=0, keepdims=True)
    cross = dot(rotated[...], turned[...], ((1,), (1,)))
    partial[...] = cross - 0.5 * level - dropped[...]


def tree_sum(values):
    while len(values) > 1:
        values = [a + b for a, b in zip(values[0::2], values[1::2])]
    return values[0]


def raise_kernel(side, used, *refs):
    parts, (raised, stats) = refs[:-2], refs[-2:]
    score = tree_sum([part[...] for part in parts])
    rows, wide = score.shape
    total = rows // side
    lane = lax.broadcasted_iota(jnp.int32, (rows, wide), 1)
    score = jnp.where(lane < used, score, NEG)
    peak = score[:total]
    for step in range(1, side):
        peak = jnp.maximum(peak, score[step * total : (step + 1) * total])
    peak = jnp.max(peak, axis=1, keepdims=True)
    added = jnp.zeros((total, wide), F32)
    for step in range(side):
        value = jnp.exp(score[step * total : (step + 1) * total] - peak)
        raised[pl.ds(step * total, total), :] = value
        added = added + value
    mass = jnp.sum(added, axis=1, keepdims=True)
    place = lax.broadcasted_iota(jnp.int32, stats.shape, 1)
    stats[...] = jnp.where(place == 0, peak, jnp.where(place == 1, mass, 0.0))


def sum_kernel(side, slots, pair, raised, own_stats, other_stats, rotated, cosine, sine, *rest):
    own_sums, own_mass, messages, moved = rest[0], rest[1], rest[2 : 1 + slots], rest[1 + slots]
    half = side // 2
    coef = cosine.shape[1]
    rows, wide = raised.shape
    total = rows // side
    owned = own_sums.shape[0]
    orient = slots * owned
    peak, mass = own_stats[:, 0:1], own_stats[:, 1:2]
    if pair > 1:
        count = total // pair
        swapped = jnp.concatenate([other_stats[count:, :], other_stats[:count, :]], axis=0)
        top = jnp.maximum(peak, swapped[:, 0:1])
        factor = jnp.exp(peak - top)
        whole = mass * factor + swapped[:, 1:2] * jnp.exp(swapped[:, 0:1] - top)
        factor = factor / whole
    else:
        factor = 1.0 / mass
    posts = []
    columns = jnp.zeros((total, wide), F32)
    for step in range(side):
        prob = raised[pl.ds(step * total, total), :] * factor
        columns = columns + prob
        posts.append(prob.astype(BF16))
    post = jnp.concatenate(posts, axis=0)
    columns = jnp.sum(columns, axis=0, keepdims=True)
    column = lax.broadcasted_iota(jnp.int32, (orient, wide), 1)
    row = lax.broadcasted_iota(jnp.int32, (orient, wide), 0)
    same = (column % orient == row) & (column < side * orient)
    masses = jnp.sum(jnp.where(same, columns, 0.0), axis=1, keepdims=True)
    spread = jnp.broadcast_to(masses, (orient, LANES))
    high = spread.astype(BF16)
    low = (spread - high.astype(F32)).astype(BF16)
    lane = lax.broadcasted_iota(jnp.int32, (orient, LANES), 1)
    tail = jnp.where(lane == 0, high.astype(F32), jnp.where(lane == 1, low.astype(F32), 0.0))
    own_mass[...] = spread[:owned]
    for slot in range(1, slots):
        piece = tail[slot * owned : (slot + 1) * owned]
        messages[slot - 1][:, pl.ds(2 * coef, LANES)] = piece.astype(BF16)

    moved[...] = dot(post, rotated[...], ((0,), (0,)))
    for start in range(0, coef, LANES):
        lanes, far = pl.ds(start, LANES), pl.ds(coef + start, LANES)

        def take(step, where):
            return moved[pl.ds((step + half) * orient, orient), where]

        real, imag = take(0, lanes), take(0, far)
        for step in range(1, half + 1):
            c = cosine[half + step - 1 : half + step, lanes]
            s = sine[half + step - 1 : half + step, lanes]
            ra, rb = take(step, lanes), take(-step, lanes)
            ia, ib = take(step, far), take(-step, far)
            real = real + (ra + rb) * c - (ia - ib) * s
            imag = imag + (ia + ib) * c + (ra - rb) * s
        own_sums[:, lanes] = real[:owned]
        own_sums[:, far] = imag[:owned]
        for slot in range(1, slots):
            part = slice(slot * owned, (slot + 1) * owned)
            messages[slot - 1][:, lanes] = real[part].astype(BF16)
            messages[slot - 1][:, far] = imag[part].astype(BF16)


def finish_kernel(own_sums, own_mass, *rest):
    messages, (sums, mass) = rest[:-2], rest[-2:]
    wide = sums.shape[1]
    owned = sums.shape[0]
    out = own_sums[...]
    level = own_mass[:, 0:1]
    for message in messages:
        out = out + message[:, pl.ds(0, wide)].astype(F32)
        tail = message[:, pl.ds(wide, LANES)].astype(F32)
        level = level + (tail[:, 0:1] + tail[:, 1:2])
    sums[...] = out
    row = lax.broadcasted_iota(jnp.int32, (owned, LANES), 0)
    lane = lax.broadcasted_iota(jnp.int32, (owned, LANES), 1)
    line = jnp.sum(jnp.where(row == lane, level, 0.0), axis=0, keepdims=True)
    mass[...] = line[:, :owned]


def call(kernel, outs, name, scratch=()):
    return pl.pallas_call(
        kernel,
        out_shape=outs,
        scratch_shapes=list(scratch),
        name=name,
        compiler_params=pltpu.CompilerParams(vmem_limit_bytes=60 * 1024 * 1024),
    )


def shaped(shape, dtype):
    return jax.ShapeDtypeStruct(shape, dtype)


def per_device(bands, places, images, references, noise_weight, masks):
    images, references, masks = images[0], references[0], masks[0]
    pair = 2 if places % 2 == 0 else 1
    slots = places // pair
    owned = references.shape[0]
    coef = noise_weight.shape[1]
    count = images.shape[0]
    side = math.isqrt(masks.shape[2])
    total = count * pair
    orient = slots * owned
    used = side * orient
    wide = round_up(used, LANES)

    def across(value, axis, size, step):
        return lax.ppermute(value, axis, [(i, i ^ step) for i in range(size)])

    far_first = list(range(slots - 1, 0, -1))
    blocks = {0: references}
    for slot in far_first:
        blocks[slot] = across(references, "img", places, slot * pair)
    if pair > 1:
        other = across(images, "img", places, 1)
        other_masks = across(masks, "img", places, 1)
    else:
        other, other_masks = images, masks

    rotated, cosine, sine, dropped = call(
        functools.partial(prepare_kernel, side, pair, slots, owned, ("band", "img")),
        (
            shaped((side * total, 2 * coef), BF16),
            shaped((8, coef), F32),
            shaped((8, coef), F32),
            shaped((side * total, wide), F32),
        ),
        "prepare",
    )(images, other, masks, other_masks)

    partial = call(
        functools.partial(score_kernel, side, slots),
        shaped((side * total, wide), F32),
        "score",
        (pltpu.VMEM((orient, 2 * coef), F32), pltpu.VMEM((wide, 2 * coef), BF16)),
    )(noise_weight, rotated, cosine, sine, dropped, *[blocks[slot] for slot in range(slots)])

    parts = {0: partial}
    for step in range(bands - 1, 0, -1):
        parts[step] = across(partial, "band", bands, step)
    raised, stats = call(
        functools.partial(raise_kernel, side, used),
        (shaped((side * total, wide), F32), shaped((total, LANES), F32)),
        "raise",
    )(*[parts[step] for step in range(bands)])
    other_stats = across(stats, "img", places, 1) if pair > 1 else stats

    outs = call(
        functools.partial(sum_kernel, side, slots, pair),
        (shaped((owned, 2 * coef), F32), shaped((owned, LANES), F32))
        + (shaped((owned, 2 * coef + LANES), BF16),) * (slots - 1),
        "sums",
        (pltpu.VMEM((wide, 2 * coef), F32),),
    )(raised, stats, other_stats, rotated, cosine, sine)
    own_sums, own_mass, messages = outs[0], outs[1], outs[2:]
    arrived = {}
    for slot in far_first:
        arrived[slot] = across(messages[slot - 1], "img", places, slot * pair)
    sums, mass = call(
        finish_kernel,
        (shaped((owned, 2 * coef), F32), shaped((1, owned), F32)),
        "finish",
    )(own_sums, own_mass, *[arrived[slot] for slot in range(1, slots)])
    return sums[None], mass[0]


def solution(mesh):
    bands, places = mesh.shape["band"], mesh.shape["img"]
    in_specs = (
        P("band", "img", None),
        P("band", "img", None),
        P("band", None),
        P("band", "img", None, None),
    )
    out_specs = (P("band", "img", None), P("img"))
    return jax.shard_map(
        functools.partial(per_device, bands, places),
        mesh=mesh,
        in_specs=in_specs,
        out_specs=out_specs,
        check_vma=False,
    )
```

```python
import functools
import math

import jax
import jax.numpy as jnp
from jax import lax
from jax.experimental import pallas as pl
from jax.experimental.pallas import tpu as pltpu
from jax.sharding import PartitionSpec as P

BOX = 256
PENALTY = 10000.0
LANES = 128
NEG = -3.0e38


F32 = jnp.float32
BF16 = jnp.bfloat16


def round_up(value, step):
    return -(-value // step) * step


def dot(a, b, dims):
    return lax.dot_general(a, b, (dims, ((), ())), preferred_element_type=F32)


def prepare_kernel(side, pair, slots, owned, axes, own, other, own_mask, other_mask, rotated, cosine, sine, dropped):
    half = side // 2
    coef = cosine.shape[1]
    band = lax.axis_index(axes[0])
    place = lax.axis_index(axes[1])

    shape = (8, coef)
    row = lax.broadcasted_iota(jnp.int32, shape, 0)
    index = lax.broadcasted_iota(jnp.int32, shape, 1)

    def modulo(value, period):
        count = jnp.floor((value.astype(F32) + 0.5) * (1.0 / period)).astype(jnp.int32)
        return value - count * period

    freq_x = modulo(index * 37 + band * 11, 257) - 128
    freq_y = modulo(index * 61 + band * 29, 129)
    phase = jnp.where(row < half, (row + 1) * freq_x, (row - half + 1) * freq_y)
    phase = jnp.bitwise_and(phase + BOX // 2, BOX - 1) - BOX // 2
    angle = phase.astype(F32) * (2.0 * math.pi / BOX)
    cosine[...] = jnp.cos(angle)
    sine[...] = jnp.sin(angle)

    count = own.shape[0]
    total = pair * count
    for part, source in enumerate((own, other)[:pair]):
        for start in range(0, coef, LANES):
            lanes, far = pl.ds(start, LANES), pl.ds(coef + start, LANES)

            def put(step, real, imag):
                rows = pl.ds((step + half) * total + part * count, count)
                rotated[rows, lanes] = real.astype(BF16)
                rotated[rows, far] = imag.astype(BF16)

            rotated[pl.ds(half * total + part * count, count), lanes] = source[:, lanes]
            rotated[pl.ds(half * total + part * count, count), far] = source[:, far]
            real = source[:, lanes].astype(F32)
            imag = source[:, far].astype(F32)
            for step in range(1, half + 1):
                c = cosine[step - 1 : step, lanes]
                s = sine[step - 1 : step, lanes]
                rc, rs, ic, iss = real * c, real * s, imag * c, imag * s
                put(step, rc - iss, rs + ic)
                put(-step, rc + iss, ic - rs)

    blocks, owners, shifts = own_mask.shape
    orient = slots * owned
    wide = dropped.shape[1]
    kept = own_mask[...].reshape(blocks * owners, shifts)
    if pair > 1:
        kept = jnp.concatenate([kept, other_mask[...].reshape(blocks * owners, shifts)], axis=0)
    gone = (1 - kept).astype(F32).astype(BF16)
    rows = kept.shape[0]
    column = lax.broadcasted_iota(jnp.int32, (shifts, wide), 1)
    shift = lax.broadcasted_iota(jnp.int32, (shifts, wide), 0)
    move_y = column // orient
    column_r = lax.broadcasted_iota(jnp.int32, (rows, wide), 1)
    row_r = lax.broadcasted_iota(jnp.int32, (rows, wide), 0)
    slot = (column_r % orient) // owned
    owner = jnp.bitwise_xor(slot, place // pair) * pair + place % pair
    mine = (row_r % owners == owner) & (column_r < side * orient)
    per_block = count // blocks
    spread = (
        lax.broadcasted_iota(jnp.int32, (total, rows), 0) // per_block
        == lax.broadcasted_iota(jnp.int32, (total, rows), 1) // owners
    )
    spread = spread.astype(F32).astype(BF16)
    for step in range(side):
        pick = ((shift == step * side + move_y) & (move_y < side)).astype(F32).astype(BF16)
        chosen = jnp.where(mine, dot(gone, pick, ((1,), (0,))), 0.0).astype(BF16)
        dropped[pl.ds(step * total, total), :] = PENALTY * dot(spread, chosen, ((1,), (0,)))


def score_kernel(side, slots, weight, rotated, cosine, sine, dropped, *rest):
    blocks, (partial, stacked, turned) = rest[:slots], rest[slots:]
    half = side // 2
    coef = cosine.shape[1]
    owned = blocks[0].shape[0]
    orient = slots * owned
    wide = partial.shape[1]
    for slot in range(slots):
        stacked[pl.ds(slot * owned, owned), :] = blocks[slot][...].astype(F32)
    if wide > side * orient:
        rest_rows = pl.ds(side * orient, wide - side * orient)
        turned[rest_rows, :] = jnp.zeros((wide - side * orient, 2 * coef), BF16)
    norms = jnp.zeros((orient, LANES), F32)
    for start in range(0, coef, LANES):
        lanes, far = pl.ds(start, LANES), pl.ds(coef + start, LANES)
        scale = weight[:, lanes]
        real, imag = stacked[:, lanes], stacked[:, far]
        norms = norms + (real * real + imag * imag) * scale
        real = (real * scale).astype(BF16)
        imag = (imag * scale).astype(BF16)

        def put(step, a, b):
            rows = pl.ds((step + half) * orient, orient)
            turned[rows, lanes] = a.astype(BF16)
            turned[rows, far] = b.astype(BF16)

        put(0, real, imag)
        real, imag = real.astype(F32), imag.astype(F32)
        for step in range(1, half + 1):
            c = cosine[half + step - 1 : half + step, lanes]
            s = sine[half + step - 1 : half + step, lanes]
            rc, rs, ic, iss = real * c, real * s, imag * c, imag * s
            put(step, rc + iss, ic - rs)
            put(-step, rc - iss, ic + rs)
    norms = jnp.sum(norms, axis=1, keepdims=True)
    column = lax.broadcasted_iota(jnp.int32, (orient, wide), 1)
    row = lax.broadcasted_iota(jnp.int32, (orient, wide), 0)
    same = (column % orient == row) & (column < side * orient)
    level = jnp.sum(jnp.where(same, norms, 0.0), axis=0, keepdims=True)
    cross = dot(rotated[...], turned[...], ((1,), (1,)))
    partial[...] = cross - 0.5 * level - dropped[...]


def tree_sum(values):
    while len(values) > 1:
        values = [a + b for a, b in zip(values[0::2], values[1::2])]
    return values[0]


def raise_kernel(side, used, *refs):
    parts, (raised, stats) = refs[:-2], refs[-2:]
    score = tree_sum([part[...] for part in parts])
    rows, wide = score.shape
    total = rows // side
    lane = lax.broadcasted_iota(jnp.int32, (rows, wide), 1)
    score = jnp.where(lane < used, score, NEG)
    peak = score[:total]
    for step in range(1, side):
        peak = jnp.maximum(peak, score[step * total : (step + 1) * total])
    peak = jnp.max(peak, axis=1, keepdims=True)
    added = jnp.zeros((total, wide), F32)
    for step in range(side):
        value = jnp.exp(score[step * total : (step + 1) * total] - peak)
        raised[pl.ds(step * total, total), :] = value
        added = added + value
    mass = jnp.sum(added, axis=1, keepdims=True)
    place = lax.broadcasted_iota(jnp.int32, stats.shape, 1)
    stats[...] = jnp.where(place == 0, peak, jnp.where(place == 1, mass, 0.0))


def sum_kernel(side, slots, pair, raised, own_stats, other_stats, rotated, cosine, sine, *rest):
    own_sums, own_mass, messages, moved = rest[0], rest[1], rest[2 : 1 + slots], rest[1 + slots]
    half = side // 2
    coef = cosine.shape[1]
    rows, wide = raised.shape
    total = rows // side
    owned = own_sums.shape[0]
    orient = slots * owned
    peak, mass = own_stats[:, 0:1], own_stats[:, 1:2]
    if pair > 1:
        count = total // pair
        swapped = jnp.concatenate([other_stats[count:, :], other_stats[:count, :]], axis=0)
        top = jnp.maximum(peak, swapped[:, 0:1])
        factor = jnp.exp(peak - top)
        whole = mass * factor + swapped[:, 1:2] * jnp.exp(swapped[:, 0:1] - top)
        factor = factor / whole
    else:
        factor = 1.0 / mass
    posts = []
    columns = jnp.zeros((total, wide), F32)
    for step in range(side):
        prob = raised[pl.ds(step * total, total), :] * factor
        columns = columns + prob
        posts.append(prob.astype(BF16))
    post = jnp.concatenate(posts, axis=0)
    columns = jnp.sum(columns, axis=0, keepdims=True)
    column = lax.broadcasted_iota(jnp.int32, (orient, wide), 1)
    row = lax.broadcasted_iota(jnp.int32, (orient, wide), 0)
    same = (column % orient == row) & (column < side * orient)
    masses = jnp.sum(jnp.where(same, columns, 0.0), axis=1, keepdims=True)
    spread = jnp.broadcast_to(masses, (orient, LANES))
    high = spread.astype(BF16)
    low = (spread - high.astype(F32)).astype(BF16)
    lane = lax.broadcasted_iota(jnp.int32, (orient, LANES), 1)
    tail = jnp.where(lane == 0, high.astype(F32), jnp.where(lane == 1, low.astype(F32), 0.0))
    own_mass[...] = spread[:owned]
    for slot in range(1, slots):
        piece = tail[slot * owned : (slot + 1) * owned]
        messages[slot - 1][:, pl.ds(2 * coef, LANES)] = piece.astype(BF16)

    moved[...] = dot(post, rotated[...], ((0,), (0,)))
    for start in range(0, coef, LANES):
        lanes, far = pl.ds(start, LANES), pl.ds(coef + start, LANES)

        def take(step, where):
            return moved[pl.ds((step + half) * orient, orient), where]

        real, imag = take(0, lanes), take(0, far)
        for step in range(1, half + 1):
            c = cosine[half + step - 1 : half + step, lanes]
            s = sine[half + step - 1 : half + step, lanes]
            ra, rb = take(step, lanes), take(-step, lanes)
            ia, ib = take(step, far), take(-step, far)
            real = real + (ra + rb) * c - (ia - ib) * s
            imag = imag + (ia + ib) * c + (ra - rb) * s
        own_sums[:, lanes] = real[:owned]
        own_sums[:, far] = imag[:owned]
        for slot in range(1, slots):
            part = slice(slot * owned, (slot + 1) * owned)
            messages[slot - 1][:, lanes] = real[part].astype(BF16)
            messages[slot - 1][:, far] = imag[part].astype(BF16)


def finish_kernel(own_sums, own_mass, *rest):
    messages, (sums, mass) = rest[:-2], rest[-2:]
    wide = sums.shape[1]
    owned = sums.shape[0]
    out = own_sums[...]
    level = own_mass[:, 0:1]
    for message in messages:
        out = out + message[:, pl.ds(0, wide)].astype(F32)
        tail = message[:, pl.ds(wide, LANES)].astype(F32)
        level = level + (tail[:, 0:1] + tail[:, 1:2])
    sums[...] = out
    row = lax.broadcasted_iota(jnp.int32, (owned, LANES), 0)
    lane = lax.broadcasted_iota(jnp.int32, (owned, LANES), 1)
    line = jnp.sum(jnp.where(row == lane, level, 0.0), axis=0, keepdims=True)
    mass[...] = line[:, :owned]


def call(kernel, outs, name, scratch=()):
    def size(value):
        return math.prod(value.shape) * jnp.dtype(value.dtype).itemsize

    def run(*args):
        held = [*args, *jax.tree.leaves(outs), *scratch]
        grant = 2 * sum(size(value) for value in held) + 4 * 1024 * 1024
        return pl.pallas_call(
            kernel,
            out_shape=outs,
            scratch_shapes=list(scratch),
            name=name,
            compiler_params=pltpu.CompilerParams(vmem_limit_bytes=min(grant, 60 * 1024 * 1024)),
        )(*args)

    return run


def shaped(shape, dtype):
    return jax.ShapeDtypeStruct(shape, dtype)


def per_device(bands, places, images, references, noise_weight, masks):
    images, references, masks = images[0], references[0], masks[0]
    pair = 2 if places % 2 == 0 else 1
    slots = places // pair
    owned = references.shape[0]
    coef = noise_weight.shape[1]
    count = images.shape[0]
    side = math.isqrt(masks.shape[2])
    total = count * pair
    orient = slots * owned
    used = side * orient
    wide = round_up(used, LANES)

    def across(value, axis, size, step):
        return lax.ppermute(value, axis, [(i, i ^ step) for i in range(size)])

    far_first = list(range(slots - 1, 0, -1))
    blocks = {0: references}
    for slot in far_first:
        blocks[slot] = across(references, "img", places, slot * pair)
    if pair > 1:
        other = across(images, "img", places, 1)
        other_masks = across(masks, "img", places, 1)
    else:
        other, other_masks = images, masks

    rotated, cosine, sine, dropped = call(
        functools.partial(prepare_kernel, side, pair, slots, owned, ("band", "img")),
        (
            shaped((side * total, 2 * coef), BF16),
            shaped((8, coef), F32),
            shaped((8, coef), F32),
            shaped((side * total, wide), F32),
        ),
        "prepare",
    )(images, other, masks, other_masks)

    partial = call(
        functools.partial(score_kernel, side, slots),
        shaped((side * total, wide), F32),
        "score",
        (pltpu.VMEM((orient, 2 * coef), F32), pltpu.VMEM((wide, 2 * coef), BF16)),
    )(noise_weight, rotated, cosine, sine, dropped, *[blocks[slot] for slot in range(slots)])

    parts = {0: partial}
    for step in range(bands - 1, 0, -1):
        parts[step] = across(partial, "band", bands, step)
    raised, stats = call(
        functools.partial(raise_kernel, side, used),
        (shaped((side * total, wide), F32), shaped((total, LANES), F32)),
        "raise",
    )(*[parts[step] for step in range(bands)])
    other_stats = across(stats, "img", places, 1) if pair > 1 else stats

    outs = call(
        functools.partial(sum_kernel, side, slots, pair),
        (shaped((owned, 2 * coef), F32), shaped((owned, LANES), F32))
        + (shaped((owned, 2 * coef + LANES), BF16),) * (slots - 1),
        "sums",
        (pltpu.VMEM((wide, 2 * coef), F32),),
    )(raised, stats, other_stats, rotated, cosine, sine)
    own_sums, own_mass, messages = outs[0], outs[1], outs[2:]
    arrived = {}
    for slot in far_first:
        arrived[slot] = across(messages[slot - 1], "img", places, slot * pair)
    sums, mass = call(
        finish_kernel,
        (shaped((owned, 2 * coef), F32), shaped((1, owned), F32)),
        "finish",
    )(own_sums, own_mass, *[arrived[slot] for slot in range(1, slots)])
    return sums[None], mass[0]


def solution(mesh):
    bands, places = mesh.shape["band"], mesh.shape["img"]
    in_specs = (
        P("band", "img", None),
        P("band", "img", None),
        P("band", None),
        P("band", "img", None, None),
    )
    out_specs = (P("band", "img", None), P("img"))
    return jax.shard_map(
        functools.partial(per_device, bands, places),
        mesh=mesh,
        in_specs=in_specs,
        out_specs=out_specs,
        check_vma=False,
    )
```

```python
import functools
import math

import jax
import jax.numpy as jnp
from jax import lax
from jax.experimental import pallas as pl
from jax.experimental.pallas import tpu as pltpu
from jax.sharding import PartitionSpec as P


BOX = 256
PENALTY = 10000.0
LANES = 128
NEG = -3.0e38


F32 = jnp.float32
BF16 = jnp.bfloat16


def round_up(value, step):
    return -(-value // step) * step


def dot(a, b, dims):
    return lax.dot_general(a, b, (dims, ((), ())), preferred_element_type=F32)


def prepare_kernel(side, pair, slots, axes, given, other, other_mask, results, scratch):
    rotated, cosine, sine, dropped, own_refs, own_weight = results
    own, own_mask, sems = scratch
    owned = own_refs.shape[0]
    copies = []
    for number, (source, target) in enumerate(zip(given, (own, own_mask, own_refs, own_weight))):
        copies.append(pltpu.make_async_copy(source, target, sems.at[number]))
        copies[-1].start()
    half = side // 2
    coef = cosine.shape[1]
    band = lax.axis_index(axes[0])
    place = lax.axis_index(axes[1])

    shape = (8, coef)
    row = lax.broadcasted_iota(jnp.int32, shape, 0)
    index = lax.broadcasted_iota(jnp.int32, shape, 1)

    def modulo(value, period):
        count = jnp.floor((value.astype(F32) + 0.5) * (1.0 / period)).astype(jnp.int32)
        return value - count * period

    freq_x = modulo(index * 37 + band * 11, 257) - 128
    freq_y = modulo(index * 61 + band * 29, 129)
    phase = jnp.where(row < half, (row + 1) * freq_x, (row - half + 1) * freq_y)
    phase = jnp.bitwise_and(phase + BOX // 2, BOX - 1) - BOX // 2
    angle = phase.astype(F32) * (2.0 * math.pi / BOX)
    cosine[...] = jnp.cos(angle)
    sine[...] = jnp.sin(angle)

    copies[0].wait()
    count = own.shape[0]
    total = pair * count
    for part, source in enumerate((own, other)[:pair]):
        for start in range(0, coef, LANES):
            lanes, far = pl.ds(start, LANES), pl.ds(coef + start, LANES)

            def put(step, real, imag):
                rows = pl.ds((step + half) * total + part * count, count)
                rotated[rows, lanes] = real.astype(BF16)
                rotated[rows, far] = imag.astype(BF16)

            rotated[pl.ds(half * total + part * count, count), lanes] = source[:, lanes]
            rotated[pl.ds(half * total + part * count, count), far] = source[:, far]
            real = source[:, lanes].astype(F32)
            imag = source[:, far].astype(F32)
            for step in range(1, half + 1):
                c = cosine[step - 1 : step, lanes]
                s = sine[step - 1 : step, lanes]
                rc, rs, ic, iss = real * c, real * s, imag * c, imag * s
                put(step, rc - iss, rs + ic)
                put(-step, rc + iss, ic - rs)

    copies[1].wait()
    blocks, owners, shifts = own_mask.shape
    orient = slots * owned
    wide = dropped.shape[1]
    kept = own_mask[...].reshape(blocks * owners, shifts)
    if pair > 1:
        kept = jnp.concatenate([kept, other_mask[...].reshape(blocks * owners, shifts)], axis=0)
    gone = (1 - kept).astype(F32).astype(BF16)
    rows = kept.shape[0]
    column = lax.broadcasted_iota(jnp.int32, (shifts, wide), 1)
    shift = lax.broadcasted_iota(jnp.int32, (shifts, wide), 0)
    move_y = column // orient
    column_r = lax.broadcasted_iota(jnp.int32, (rows, wide), 1)
    row_r = lax.broadcasted_iota(jnp.int32, (rows, wide), 0)
    slot = (column_r % orient) // owned
    owner = jnp.bitwise_xor(slot, place // pair) * pair + place % pair
    mine = (row_r % owners == owner) & (column_r < side * orient)
    per_block = count // blocks
    spread = (
        lax.broadcasted_iota(jnp.int32, (total, rows), 0) // per_block
        == lax.broadcasted_iota(jnp.int32, (total, rows), 1) // owners
    )
    spread = spread.astype(F32).astype(BF16)
    for step in range(side):
        pick = ((shift == step * side + move_y) & (move_y < side)).astype(F32).astype(BF16)
        chosen = jnp.where(mine, dot(gone, pick, ((1,), (0,))), 0.0).astype(BF16)
        dropped[pl.ds(step * total, total), :] = PENALTY * dot(spread, chosen, ((1,), (0,)))
    copies[2].wait()
    copies[3].wait()


def score_kernel(side, slots, weight, rotated, cosine, sine, dropped, *rest):
    blocks, (partial, stacked, turned) = rest[:slots], rest[slots:]
    half = side // 2
    coef = cosine.shape[1]
    owned = blocks[0].shape[0]
    orient = slots * owned
    wide = partial.shape[1]
    for slot in range(slots):
        stacked[pl.ds(slot * owned, owned), :] = blocks[slot][...].astype(F32)
    if wide > side * orient:
        rest_rows = pl.ds(side * orient, wide - side * orient)
        turned[rest_rows, :] = jnp.zeros((wide - side * orient, 2 * coef), BF16)
    norms = jnp.zeros((orient, LANES), F32)
    for start in range(0, coef, LANES):
        lanes, far = pl.ds(start, LANES), pl.ds(coef + start, LANES)
        scale = weight[:, lanes]
        real, imag = stacked[:, lanes], stacked[:, far]
        norms = norms + (real * real + imag * imag) * scale
        real = (real * scale).astype(BF16)
        imag = (imag * scale).astype(BF16)

        def put(step, a, b):
            rows = pl.ds((step + half) * orient, orient)
            turned[rows, lanes] = a.astype(BF16)
            turned[rows, far] = b.astype(BF16)

        put(0, real, imag)
        real, imag = real.astype(F32), imag.astype(F32)
        for step in range(1, half + 1):
            c = cosine[half + step - 1 : half + step, lanes]
            s = sine[half + step - 1 : half + step, lanes]
            rc, rs, ic, iss = real * c, real * s, imag * c, imag * s
            put(step, rc + iss, ic - rs)
            put(-step, rc - iss, ic + rs)
    norms = jnp.sum(norms, axis=1, keepdims=True)
    column = lax.broadcasted_iota(jnp.int32, (orient, wide), 1)
    row = lax.broadcasted_iota(jnp.int32, (orient, wide), 0)
    same = (column % orient == row) & (column < side * orient)
    level = jnp.sum(jnp.where(same, norms, 0.0), axis=0, keepdims=True)
    cross = dot(rotated[...], turned[...], ((1,), (1,)))
    partial[...] = cross - 0.5 * level - dropped[...]


def tree_sum(values):
    while len(values) > 1:
        values = [a + b for a, b in zip(values[0::2], values[1::2])]
    return values[0]


def raise_kernel(side, used, *refs):
    parts, (raised, stats) = refs[:-2], refs[-2:]
    score = tree_sum([part[...] for part in parts])
    rows, wide = score.shape
    total = rows // side
    lane = lax.broadcasted_iota(jnp.int32, (rows, wide), 1)
    score = jnp.where(lane < used, score, NEG)
    peak = score[:total]
    for step in range(1, side):
        peak = jnp.maximum(peak, score[step * total : (step + 1) * total])
    peak = jnp.max(peak, axis=1, keepdims=True)
    added = jnp.zeros((total, wide), F32)
    for step in range(side):
        value = jnp.exp(score[step * total : (step + 1) * total] - peak)
        raised[pl.ds(step * total, total), :] = value
        added = added + value
    mass = jnp.sum(added, axis=1, keepdims=True)
    place = lax.broadcasted_iota(jnp.int32, stats.shape, 1)
    stats[...] = jnp.where(place == 0, peak, jnp.where(place == 1, mass, 0.0))


def sum_kernel(side, slots, pair, raised, own_stats, other_stats, rotated, cosine, sine, *rest):
    own_sums, own_mass, messages, moved = rest[0], rest[1], rest[2 : 1 + slots], rest[1 + slots]
    half = side // 2
    coef = cosine.shape[1]
    rows, wide = raised.shape
    total = rows // side
    owned = own_sums.shape[0]
    orient = slots * owned
    peak, mass = own_stats[:, 0:1], own_stats[:, 1:2]
    if pair > 1:
        count = total // pair
        swapped = jnp.concatenate([other_stats[count:, :], other_stats[:count, :]], axis=0)
        top = jnp.maximum(peak, swapped[:, 0:1])
        factor = jnp.exp(peak - top)
        whole = mass * factor + swapped[:, 1:2] * jnp.exp(swapped[:, 0:1] - top)
        factor = factor / whole
    else:
        factor = 1.0 / mass
    posts = []
    columns = jnp.zeros((total, wide), F32)
    for step in range(side):
        prob = raised[pl.ds(step * total, total), :] * factor
        columns = columns + prob
        posts.append(prob.astype(BF16))
    post = jnp.concatenate(posts, axis=0)
    columns = jnp.sum(columns, axis=0, keepdims=True)
    column = lax.broadcasted_iota(jnp.int32, (orient, wide), 1)
    row = lax.broadcasted_iota(jnp.int32, (orient, wide), 0)
    same = (column % orient == row) & (column < side * orient)
    masses = jnp.sum(jnp.where(same, columns, 0.0), axis=1, keepdims=True)
    spread = jnp.broadcast_to(masses, (orient, LANES))
    high = spread.astype(BF16)
    low = (spread - high.astype(F32)).astype(BF16)
    lane = lax.broadcasted_iota(jnp.int32, (orient, LANES), 1)
    tail = jnp.where(lane == 0, high.astype(F32), jnp.where(lane == 1, low.astype(F32), 0.0))
    own_mass[...] = spread[:owned]
    for slot in range(1, slots):
        piece = tail[slot * owned : (slot + 1) * owned]
        messages[slot - 1][:, pl.ds(2 * coef, LANES)] = piece.astype(BF16)

    moved[...] = dot(post, rotated[...], ((0,), (0,)))
    for start in range(0, coef, LANES):
        lanes, far = pl.ds(start, LANES), pl.ds(coef + start, LANES)

        def take(step, where):
            return moved[pl.ds((step + half) * orient, orient), where]

        real, imag = take(0, lanes), take(0, far)
        for step in range(1, half + 1):
            c = cosine[half + step - 1 : half + step, lanes]
            s = sine[half + step - 1 : half + step, lanes]
            ra, rb = take(step, lanes), take(-step, lanes)
            ia, ib = take(step, far), take(-step, far)
            real = real + (ra + rb) * c - (ia - ib) * s
            imag = imag + (ia + ib) * c + (ra - rb) * s
        own_sums[:, lanes] = real[:owned]
        own_sums[:, far] = imag[:owned]
        for slot in range(1, slots):
            part = slice(slot * owned, (slot + 1) * owned)
            messages[slot - 1][:, lanes] = real[part].astype(BF16)
            messages[slot - 1][:, far] = imag[part].astype(BF16)


def finish_kernel(own_sums, own_mass, *rest):
    messages, (sums, mass) = rest[:-2], rest[-2:]
    wide = sums.shape[1]
    owned = sums.shape[0]
    out = own_sums[...]
    level = own_mass[:, 0:1]
    for message in messages:
        out = out + message[:, pl.ds(0, wide)].astype(F32)
        tail = message[:, pl.ds(wide, LANES)].astype(F32)
        level = level + (tail[:, 0:1] + tail[:, 1:2])
    sums[...] = out
    row = lax.broadcasted_iota(jnp.int32, (owned, LANES), 0)
    lane = lax.broadcasted_iota(jnp.int32, (owned, LANES), 1)
    line = jnp.sum(jnp.where(row == lane, level, 0.0), axis=0, keepdims=True)
    mass[...] = line[:, :owned]


def call(kernel, outs, scratch=(), far=0):
    def size(value):
        return math.prod(value.shape) * jnp.dtype(value.dtype).itemsize

    def run(*args):
        held = [*args, *jax.tree.leaves(outs), *[value for value in scratch if value.memory_space == pltpu.MemorySpace.VMEM]]
        grant = 2 * sum(size(value) for value in held) + 4 * 1024 * 1024
        spaces = [pltpu.MemorySpace.HBM] * far + [pltpu.MemorySpace.VMEM] * (len(args) - far)
        return pl.pallas_call(
            kernel,
            in_specs=[pl.BlockSpec(memory_space=space) for space in spaces],
            out_shape=outs,
            scratch_shapes=list(scratch),
            compiler_params=pltpu.CompilerParams(vmem_limit_bytes=min(grant, 60 * 1024 * 1024)),
        )(*args)

    return run


def shaped(shape, dtype):
    return jax.ShapeDtypeStruct(shape, dtype)


def per_device(bands, places, images, references, noise_weight, masks):
    images, references, masks = images[0], references[0], masks[0]
    pair = 2 if places % 2 == 0 else 1
    slots = places // pair
    owned = references.shape[0]
    coef = noise_weight.shape[1]
    count = images.shape[0]
    side = math.isqrt(masks.shape[2])
    total = count * pair
    orient = slots * owned
    used = side * orient
    wide = round_up(used, LANES)

    def across(value, axis, size, step):
        return lax.ppermute(value, axis, [(i, i ^ step) for i in range(size)])

    far_first = list(range(slots - 1, 0, -1))
    blocks = {}
    if pair > 1:
        other = across(images, "img", places, 1)
        other_masks = across(masks, "img", places, 1)
    else:
        other, other_masks = images, masks
    for slot in far_first:
        blocks[slot] = across(references, "img", places, slot * pair)

    def prepare(*refs):
        given, refs = refs[:4], refs[4:]
        prepare_kernel(side, pair, slots, ("band", "img"), given, refs[0], refs[1], refs[2:8], refs[8:])

    rotated, cosine, sine, dropped, blocks[0], weight = call(
        prepare,
        (
            shaped((side * total, 2 * coef), BF16),
            shaped((8, coef), F32),
            shaped((8, coef), F32),
            shaped((side * total, wide), F32),
            shaped(references.shape, references.dtype),
            shaped(noise_weight.shape, noise_weight.dtype),
        ),
        (
            pltpu.VMEM(images.shape, images.dtype),
            pltpu.VMEM(masks.shape, masks.dtype),
            pltpu.SemaphoreType.DMA((4,)),
        ),
        4,
    )(*[pltpu.with_memory_space_constraint(value, pltpu.MemorySpace.HBM) for value in (images, masks, references, noise_weight)], other, other_masks)

    partial = call(
        functools.partial(score_kernel, side, slots),
        shaped((side * total, wide), F32),
        (pltpu.VMEM((orient, 2 * coef), F32), pltpu.VMEM((wide, 2 * coef), BF16)),
    )(weight, rotated, cosine, sine, dropped, *[blocks[slot] for slot in range(slots)])

    parts = {0: partial}
    for step in range(bands - 1, 0, -1):
        parts[step] = across(partial, "band", bands, step)
    raised, stats = call(
        functools.partial(raise_kernel, side, used),
        (shaped((side * total, wide), F32), shaped((total, LANES), F32)),
    )(*[parts[step] for step in range(bands)])
    other_stats = across(stats, "img", places, 1) if pair > 1 else stats

    outs = call(
        functools.partial(sum_kernel, side, slots, pair),
        (shaped((owned, 2 * coef), F32), shaped((owned, LANES), F32))
        + (shaped((owned, 2 * coef + LANES), BF16),) * (slots - 1),
        (pltpu.VMEM((wide, 2 * coef), F32),),
    )(raised, stats, other_stats, rotated, cosine, sine)
    own_sums, own_mass, messages = outs[0], outs[1], outs[2:]
    arrived = {}
    for slot in far_first:
        arrived[slot] = across(messages[slot - 1], "img", places, slot * pair)
    sums, mass = call(
        finish_kernel, (shaped((owned, 2 * coef), F32), shaped((1, owned), F32))
    )(own_sums, own_mass, *[arrived[slot] for slot in range(1, slots)])
    return sums[None], mass[0]


def solution(mesh):
    bands, places = mesh.shape["band"], mesh.shape["img"]
    in_specs = (
        P("band", "img", None),
        P("band", "img", None),
        P("band", None),
        P("band", "img", None, None),
    )
    out_specs = (P("band", "img", None), P("img"))

    def body(*args):
        return per_device(bands, places, *args)

    return jax.shard_map(body, mesh=mesh, in_specs=in_specs, out_specs=out_specs, check_vma=False)
```

```python
import functools
import math

import jax
import jax.numpy as jnp
from jax import lax
from jax.experimental import pallas as pl
from jax.experimental.pallas import tpu as pltpu
from jax.sharding import PartitionSpec as P


BOX = 256
PENALTY = 10000.0
LANES = 128
NEG = -3.0e38


F32 = jnp.float32
BF16 = jnp.bfloat16


def round_up(value, step):
    return -(-value // step) * step


def divided(value, by):
    if by & (by - 1) == 0:
        return lax.shift_right_logical(value, jnp.int32(by.bit_length() - 1)), value & (by - 1)
    quotient = jnp.floor((value.astype(F32) + 0.5) * (1.0 / by)).astype(jnp.int32)
    return quotient, value - quotient * by


def dot(a, b, dims):
    return lax.dot_general(a, b, (dims, ((), ())), preferred_element_type=F32)


def prepare_kernel(side, pair, slots, axes, given, other, other_mask, results, scratch):
    rotated, cosine, sine, dropped, own_refs, own_weight = results
    own, own_mask, sems = scratch
    owned = own_refs.shape[0]
    copies = []
    for number, (source, target) in enumerate(zip(given, (own, own_mask, own_refs, own_weight))):
        copies.append(pltpu.make_async_copy(source, target, sems.at[number]))
        copies[-1].start()
    half = side // 2
    coef = cosine.shape[1]
    band = lax.axis_index(axes[0])
    place = lax.axis_index(axes[1])

    shape = (8, coef)
    row = lax.broadcasted_iota(jnp.int32, shape, 0)
    index = lax.broadcasted_iota(jnp.int32, shape, 1)

    freq_x = divided(index * 37 + band * 11, 257)[1] - 128
    freq_y = divided(index * 61 + band * 29, 129)[1]
    phase = jnp.where(row < half, (row + 1) * freq_x, (row - half + 1) * freq_y)
    phase = jnp.bitwise_and(phase + BOX // 2, BOX - 1) - BOX // 2
    angle = phase.astype(F32) * (2.0 * math.pi / BOX)
    cosine[...] = jnp.cos(angle)
    sine[...] = jnp.sin(angle)

    copies[0].wait()
    count = own.shape[0]
    total = pair * count
    for part, source in enumerate((own, other)[:pair]):
        for start in range(0, coef, LANES):
            lanes, far = pl.ds(start, LANES), pl.ds(coef + start, LANES)

            def put(step, real, imag):
                rows = pl.ds((step + half) * total + part * count, count)
                rotated[rows, lanes] = real.astype(BF16)
                rotated[rows, far] = imag.astype(BF16)

            rotated[pl.ds(half * total + part * count, count), lanes] = source[:, lanes]
            rotated[pl.ds(half * total + part * count, count), far] = source[:, far]
            real = source[:, lanes].astype(F32)
            imag = source[:, far].astype(F32)
            for step in range(1, half + 1):
                c = cosine[step - 1 : step, lanes]
                s = sine[step - 1 : step, lanes]
                rc, rs, ic, iss = real * c, real * s, imag * c, imag * s
                put(step, rc - iss, rs + ic)
                put(-step, rc + iss, ic - rs)

    copies[1].wait()
    blocks, owners, shifts = own_mask.shape
    orient = slots * owned
    wide = dropped.shape[1]
    kept = own_mask[...].reshape(blocks * owners, shifts)
    if pair > 1:
        kept = jnp.concatenate([kept, other_mask[...].reshape(blocks * owners, shifts)], axis=0)
    gone = (1 - kept).astype(F32).astype(BF16)
    rows = kept.shape[0]

    def iota(shape, dim):
        return lax.broadcasted_iota(jnp.int32, shape, dim)

    step, column = divided(iota((1, side * wide), 1), wide)
    move_y, place_o = divided(column, orient)
    slot = divided(place_o, owned)[0]
    used = move_y < side
    wanted = jnp.where(used, step * side + move_y, -1)
    pick = (iota((shifts, side * wide), 0) == wanted).astype(F32).astype(BF16)
    owner = jnp.bitwise_xor(slot, place // pair) * pair + place % pair
    mine = divided(iota((rows, 1), 0), owners)[1] == owner
    spread = divided(iota((total, 1), 0), count // blocks)[0] == divided(iota((1, rows), 1), owners)[0]
    spread = spread.astype(F32).astype(BF16)
    chosen = jnp.where(mine, dot(gone, pick, ((1,), (0,))), 0.0).astype(BF16)
    level = PENALTY * dot(spread, chosen, ((1,), (0,)))
    for step in range(side):
        dropped[pl.ds(step * total, total), :] = level[:, step * wide : (step + 1) * wide]
    copies[2].wait()
    copies[3].wait()


def score_kernel(side, slots, weight, rotated, cosine, sine, dropped, *rest):
    blocks, (partial, stacked, turned) = rest[:slots], rest[slots:]
    half = side // 2
    coef = cosine.shape[1]
    owned = blocks[0].shape[0]
    orient = slots * owned
    wide = partial.shape[1]
    for slot in range(slots):
        stacked[pl.ds(slot * owned, owned), :] = blocks[slot][...].astype(F32)
    if wide > side * orient:
        rest_rows = pl.ds(side * orient, wide - side * orient)
        turned[rest_rows, :] = jnp.zeros((wide - side * orient, 2 * coef), BF16)
    norms = jnp.zeros((orient, LANES), F32)
    for start in range(0, coef, LANES):
        lanes, far = pl.ds(start, LANES), pl.ds(coef + start, LANES)
        scale = weight[:, lanes]
        real, imag = stacked[:, lanes], stacked[:, far]
        norms = norms + (real * real + imag * imag) * scale
        real = (real * scale).astype(BF16)
        imag = (imag * scale).astype(BF16)

        def put(step, a, b):
            rows = pl.ds((step + half) * orient, orient)
            turned[rows, lanes] = a.astype(BF16)
            turned[rows, far] = b.astype(BF16)

        put(0, real, imag)
        real, imag = real.astype(F32), imag.astype(F32)
        for step in range(1, half + 1):
            c = cosine[half + step - 1 : half + step, lanes]
            s = sine[half + step - 1 : half + step, lanes]
            rc, rs, ic, iss = real * c, real * s, imag * c, imag * s
            put(step, rc + iss, ic - rs)
            put(-step, rc - iss, ic + rs)
    norms = jnp.sum(norms, axis=1, keepdims=True)
    column = lax.broadcasted_iota(jnp.int32, (orient, wide), 1)
    row = lax.broadcasted_iota(jnp.int32, (orient, wide), 0)
    same = (divided(column, orient)[1] == row) & (column < side * orient)
    level = jnp.sum(jnp.where(same, norms, 0.0), axis=0, keepdims=True)
    cross = dot(rotated[...], turned[...], ((1,), (1,)))
    partial[...] = cross - 0.5 * level - dropped[...]


def tree_sum(values):
    while len(values) > 1:
        values = [a + b for a, b in zip(values[0::2], values[1::2])]
    return values[0]


def raise_kernel(side, used, *refs):
    parts, (raised, stats) = refs[:-2], refs[-2:]
    score = tree_sum([part[...] for part in parts])
    rows, wide = score.shape
    total = rows // side
    lane = lax.broadcasted_iota(jnp.int32, (rows, wide), 1)
    score = jnp.where(lane < used, score, NEG)
    peak = score[:total]
    for step in range(1, side):
        peak = jnp.maximum(peak, score[step * total : (step + 1) * total])
    peak = jnp.max(peak, axis=1, keepdims=True)
    added = jnp.zeros((total, wide), F32)
    for step in range(side):
        value = jnp.exp(score[step * total : (step + 1) * total] - peak)
        raised[pl.ds(step * total, total), :] = value
        added = added + value
    mass = jnp.sum(added, axis=1, keepdims=True)
    place = lax.broadcasted_iota(jnp.int32, stats.shape, 1)
    stats[...] = jnp.where(place == 0, peak, jnp.where(place == 1, mass, 0.0))


def sum_kernel(side, slots, pair, raised, own_stats, other_stats, rotated, cosine, sine, *rest):
    own_sums, own_mass, messages, moved = rest[0], rest[1], rest[2 : 1 + slots], rest[1 + slots]
    half = side // 2
    coef = cosine.shape[1]
    rows, wide = raised.shape
    total = rows // side
    owned = own_sums.shape[0]
    orient = slots * owned
    peak, mass = own_stats[:, 0:1], own_stats[:, 1:2]
    if pair > 1:
        count = total // pair
        swapped = jnp.concatenate([other_stats[count:, :], other_stats[:count, :]], axis=0)
        top = jnp.maximum(peak, swapped[:, 0:1])
        factor = jnp.exp(peak - top)
        whole = mass * factor + swapped[:, 1:2] * jnp.exp(swapped[:, 0:1] - top)
        factor = factor / whole
    else:
        factor = 1.0 / mass
    posts = []
    columns = jnp.zeros((total, wide), F32)
    for step in range(side):
        prob = raised[pl.ds(step * total, total), :] * factor
        columns = columns + prob
        posts.append(prob.astype(BF16))
    post = jnp.concatenate(posts, axis=0)
    columns = jnp.sum(columns, axis=0, keepdims=True)
    column = lax.broadcasted_iota(jnp.int32, (orient, wide), 1)
    row = lax.broadcasted_iota(jnp.int32, (orient, wide), 0)
    same = (divided(column, orient)[1] == row) & (column < side * orient)
    masses = jnp.sum(jnp.where(same, columns, 0.0), axis=1, keepdims=True)
    spread = jnp.broadcast_to(masses, (orient, LANES))
    high = spread.astype(BF16)
    low = (spread - high.astype(F32)).astype(BF16)
    lane = lax.broadcasted_iota(jnp.int32, (orient, LANES), 1)
    tail = jnp.where(lane == 0, high.astype(F32), jnp.where(lane == 1, low.astype(F32), 0.0))
    own_mass[...] = spread[:owned]
    for slot in range(1, slots):
        piece = tail[slot * owned : (slot + 1) * owned]
        messages[slot - 1][:, pl.ds(2 * coef, LANES)] = piece.astype(BF16)

    moved[...] = dot(post, rotated[...], ((0,), (0,)))
    for start in range(0, coef, LANES):
        lanes, far = pl.ds(start, LANES), pl.ds(coef + start, LANES)

        def take(step, where):
            return moved[pl.ds((step + half) * orient, orient), where]

        real, imag = take(0, lanes), take(0, far)
        for step in range(1, half + 1):
            c = cosine[half + step - 1 : half + step, lanes]
            s = sine[half + step - 1 : half + step, lanes]
            ra, rb = take(step, lanes), take(-step, lanes)
            ia, ib = take(step, far), take(-step, far)
            real = real + (ra + rb) * c - (ia - ib) * s
            imag = imag + (ia + ib) * c + (ra - rb) * s
        own_sums[:, lanes] = real[:owned]
        own_sums[:, far] = imag[:owned]
        for slot in range(1, slots):
            part = slice(slot * owned, (slot + 1) * owned)
            messages[slot - 1][:, lanes] = real[part].astype(BF16)
            messages[slot - 1][:, far] = imag[part].astype(BF16)


def finish_kernel(own_sums, own_mass, *rest):
    messages, (sums, mass) = rest[:-2], rest[-2:]
    wide = sums.shape[1]
    owned = sums.shape[0]
    out = own_sums[...]
    level = own_mass[:, 0:1]
    for message in messages:
        out = out + message[:, pl.ds(0, wide)].astype(F32)
        tail = message[:, pl.ds(wide, LANES)].astype(F32)
        level = level + (tail[:, 0:1] + tail[:, 1:2])
    sums[...] = out
    row = lax.broadcasted_iota(jnp.int32, (owned, LANES), 0)
    lane = lax.broadcasted_iota(jnp.int32, (owned, LANES), 1)
    line = jnp.sum(jnp.where(row == lane, level, 0.0), axis=0, keepdims=True)
    mass[...] = line[:, :owned]


def call(kernel, outs, scratch=(), far=0):
    def size(value):
        return math.prod(value.shape) * jnp.dtype(value.dtype).itemsize

    def run(*args):
        held = [*args, *jax.tree.leaves(outs), *[value for value in scratch if value.memory_space == pltpu.MemorySpace.VMEM]]
        grant = 2 * sum(size(value) for value in held) + 4 * 1024 * 1024
        spaces = [pltpu.MemorySpace.HBM] * far + [pltpu.MemorySpace.VMEM] * (len(args) - far)
        return pl.pallas_call(
            kernel,
            in_specs=[pl.BlockSpec(memory_space=space) for space in spaces],
            out_shape=outs,
            scratch_shapes=list(scratch),
            compiler_params=pltpu.CompilerParams(vmem_limit_bytes=min(grant, 60 * 1024 * 1024)),
        )(*args)

    return run


def shaped(shape, dtype):
    return jax.ShapeDtypeStruct(shape, dtype)


def per_device(bands, places, images, references, noise_weight, masks):
    images, references, masks = images[0], references[0], masks[0]
    pair = 2 if places % 2 == 0 else 1
    slots = places // pair
    owned = references.shape[0]
    coef = noise_weight.shape[1]
    count = images.shape[0]
    side = math.isqrt(masks.shape[2])
    total = count * pair
    orient = slots * owned
    used = side * orient
    wide = round_up(used, LANES)

    def across(value, axis, size, step):
        return lax.ppermute(value, axis, [(i, i ^ step) for i in range(size)])

    far_first = list(range(slots - 1, 0, -1))
    blocks = {}
    if pair > 1:
        other = across(images, "img", places, 1)
        other_masks = across(masks, "img", places, 1)
    else:
        other, other_masks = images, masks
    for slot in far_first:
        blocks[slot] = across(references, "img", places, slot * pair)

    def far_away(value):
        return pltpu.with_memory_space_constraint(value, pltpu.MemorySpace.HBM)

    def prepare(*refs):
        given, refs = refs[:4], refs[4:]
        prepare_kernel(side, pair, slots, ("band", "img"), given, refs[0], refs[1], refs[2:8], refs[8:])

    rotated, cosine, sine, dropped, blocks[0], weight = call(
        prepare,
        (
            shaped((side * total, 2 * coef), BF16),
            shaped((8, coef), F32),
            shaped((8, coef), F32),
            shaped((side * total, wide), F32),
            shaped(references.shape, references.dtype),
            shaped(noise_weight.shape, noise_weight.dtype),
        ),
        (
            pltpu.VMEM(images.shape, images.dtype),
            pltpu.VMEM(masks.shape, masks.dtype),
            pltpu.SemaphoreType.DMA((4,)),
        ),
        4,
    )(*[far_away(value) for value in (images, masks, references, noise_weight)], other, other_masks)

    partial = call(
        functools.partial(score_kernel, side, slots),
        shaped((side * total, wide), F32),
        (pltpu.VMEM((orient, 2 * coef), F32), pltpu.VMEM((wide, 2 * coef), BF16)),
    )(weight, rotated, cosine, sine, dropped, *[blocks[slot] for slot in range(slots)])

    parts = {0: partial}
    for step in range(bands - 1, 0, -1):
        parts[step] = across(partial, "band", bands, step)
    raised, stats = call(
        functools.partial(raise_kernel, side, used),
        (shaped((side * total, wide), F32), shaped((total, LANES), F32)),
    )(*[parts[step] for step in range(bands)])
    other_stats = across(stats, "img", places, 1) if pair > 1 else stats

    outs = call(
        functools.partial(sum_kernel, side, slots, pair),
        (shaped((owned, 2 * coef), F32), shaped((owned, LANES), F32))
        + (shaped((owned, 2 * coef + LANES), BF16),) * (slots - 1),
        (pltpu.VMEM((wide, 2 * coef), F32),),
    )(raised, stats, other_stats, rotated, cosine, sine)
    own_sums, own_mass, messages = outs[0], outs[1], outs[2:]
    arrived = {}
    for slot in far_first:
        arrived[slot] = across(messages[slot - 1], "img", places, slot * pair)
    sums, mass = call(
        finish_kernel, (shaped((owned, 2 * coef), F32), shaped((1, owned), F32))
    )(own_sums, own_mass, *[arrived[slot] for slot in range(1, slots)])
    return sums[None], mass[0]


def solution(mesh):
    bands, places = mesh.shape["band"], mesh.shape["img"]
    in_specs = (
        P("band", "img", None),
        P("band", "img", None),
        P("band", None),
        P("band", "img", None, None),
    )
    out_specs = (P("band", "img", None), P("img"))

    def body(*args):
        return per_device(bands, places, *args)

    return jax.shard_map(body, mesh=mesh, in_specs=in_specs, out_specs=out_specs, check_vma=False)
```

```python
import functools
import math

import jax
import jax.numpy as jnp
from jax import lax
from jax.experimental import pallas as pl
from jax.experimental.pallas import tpu as pltpu
from jax.sharding import PartitionSpec as P


BOX = 256
PENALTY = 10000.0
LANES = 128
NEG = -3.0e38
TINY = 1.0e-30
STEPS = 32767.0


F32 = jnp.float32
BF16 = jnp.bfloat16


def round_up(value, step):
    return -(-value // step) * step


def divided(value, by):
    if by & (by - 1) == 0:
        return lax.shift_right_logical(value, jnp.int32(by.bit_length() - 1)), value & (by - 1)
    quotient = jnp.floor((value.astype(F32) + 0.5) * (1.0 / by)).astype(jnp.int32)
    return quotient, value - quotient * by


def dot(a, b, dims):
    return lax.dot_general(a, b, (dims, ((), ())), preferred_element_type=F32)


def prepare_kernel(side, pair, slots, owned, axes, given, other, other_mask, results, scratch):
    rotated, cosine, sine, dropped, own_weight = results
    own, own_mask, sems = scratch
    copies = []
    for number, (source, target) in enumerate(zip(given, (own, own_mask, own_weight))):
        copies.append(pltpu.make_async_copy(source, target, sems.at[number]))
        copies[-1].start()
    half = side // 2
    coef = cosine.shape[1]
    band = lax.axis_index(axes[0])
    place = lax.axis_index(axes[1])

    shape = (8, coef)
    row = lax.broadcasted_iota(jnp.int32, shape, 0)
    index = lax.broadcasted_iota(jnp.int32, shape, 1)

    freq_x = divided(index * 37 + band * 11, 257)[1] - 128
    freq_y = divided(index * 61 + band * 29, 129)[1]
    phase = jnp.where(row < half, (row + 1) * freq_x, (row - half + 1) * freq_y)
    phase = jnp.bitwise_and(phase + BOX // 2, BOX - 1) - BOX // 2
    angle = phase.astype(F32) * (2.0 * math.pi / BOX)
    cosine[...] = jnp.cos(angle)
    sine[...] = jnp.sin(angle)

    count = own.shape[0]
    total = pair * count
    for part, source in reversed(list(enumerate((own, other)[:pair]))):
        if part == 0:
            copies[0].wait()
        for start in range(0, coef, LANES):
            lanes, far = pl.ds(start, LANES), pl.ds(coef + start, LANES)

            def put(step, real, imag):
                rows = pl.ds((step + half) * total + part * count, count)
                rotated[rows, lanes] = real.astype(BF16)
                rotated[rows, far] = imag.astype(BF16)

            rotated[pl.ds(half * total + part * count, count), lanes] = source[:, lanes]
            rotated[pl.ds(half * total + part * count, count), far] = source[:, far]
            real = source[:, lanes].astype(F32)
            imag = source[:, far].astype(F32)
            for step in range(1, half + 1):
                c = cosine[step - 1 : step, lanes]
                s = sine[step - 1 : step, lanes]
                rc, rs, ic, iss = real * c, real * s, imag * c, imag * s
                put(step, rc - iss, rs + ic)
                put(-step, rc + iss, ic - rs)

    copies[1].wait()
    blocks, owners, shifts = own_mask.shape
    orient = slots * owned
    wide = dropped.shape[1]
    kept = own_mask[...].reshape(blocks * owners, shifts)
    if pair > 1:
        kept = jnp.concatenate([kept, other_mask[...].reshape(blocks * owners, shifts)], axis=0)
    gone = (1 - kept).astype(F32).astype(BF16)
    rows = kept.shape[0]

    def iota(shape, dim):
        return lax.broadcasted_iota(jnp.int32, shape, dim)

    step, column = divided(iota((1, side * wide), 1), wide)
    move_y, place_o = divided(column, orient)
    slot = divided(place_o, owned)[0]
    used = move_y < side
    wanted = jnp.where(used, step * side + move_y, -1)
    pick = (iota((shifts, side * wide), 0) == wanted).astype(F32).astype(BF16)
    owner = jnp.bitwise_xor(slot * pair + pair - 1, place)
    mine = divided(iota((rows, 1), 0), owners)[1] == owner
    groups = pair * blocks
    spread = iota((groups, 1), 0) == divided(iota((1, rows), 1), owners)[0]
    spread = spread.astype(F32).astype(BF16)
    chosen = jnp.where(mine, dot(gone, pick, ((1,), (0,))), 0.0).astype(BF16)
    level = dot(spread, chosen, ((1,), (0,)))
    dropped[...] = jnp.concatenate([level[:, step * wide : (step + 1) * wide] for step in range(side)], axis=0)
    copies[2].wait()


def score_kernel(side, weight, rotated, cosine, sine, dropped, *rest):
    blocks, partial = rest[:-1], rest[-1]
    half = side // 2
    coef = cosine.shape[1]
    orient = len(blocks) * blocks[0].shape[0]
    rows, wide = rotated.shape[0], partial.shape[1]
    norms = jnp.zeros((orient, LANES), F32)
    cross = jnp.zeros((rows, wide), F32)
    for start in range(0, coef, LANES):
        lanes, far = pl.ds(start, LANES), pl.ds(coef + start, LANES)
        scale = weight[:, lanes]
        real = jnp.concatenate([block[:, lanes].astype(F32) for block in blocks], axis=0)
        imag = jnp.concatenate([block[:, far].astype(F32) for block in blocks], axis=0)
        norms = norms + (real * real + imag * imag) * scale
        pieces = {0: ((real * scale).astype(BF16), (imag * scale).astype(BF16))}
        real, imag = pieces[0][0].astype(F32), pieces[0][1].astype(F32)
        for step in range(1, half + 1):
            c = cosine[half + step - 1 : half + step, lanes]
            s = sine[half + step - 1 : half + step, lanes]
            rc, rs, ic, iss = real * c, real * s, imag * c, imag * s
            pieces[step] = ((rc + iss).astype(BF16), (ic - rs).astype(BF16))
            pieces[-step] = ((rc - iss).astype(BF16), (ic + rs).astype(BF16))
        turned = [jnp.concatenate(pieces[step - half], axis=1) for step in range(side)]
        if wide > side * orient:
            turned.append(jnp.zeros((wide - side * orient, 2 * LANES), BF16))
        turned = jnp.concatenate(turned, axis=0)
        images = jnp.concatenate([rotated[:, lanes], rotated[:, far]], axis=1)
        cross = cross + dot(images, turned, ((1,), (1,)))
    norms = jnp.sum(norms, axis=1, keepdims=True)
    column = lax.broadcasted_iota(jnp.int32, (orient, wide), 1)
    row = lax.broadcasted_iota(jnp.int32, (orient, wide), 0)
    same = (divided(column, orient)[1] == row) & (column < side * orient)
    level = jnp.sum(jnp.where(same, norms, 0.0), axis=0, keepdims=True)
    value = cross - 0.5 * level
    used = side * orient
    lane = lax.broadcasted_iota(jnp.int32, (rows, wide), 1)
    largest = jnp.max(jnp.where(lane < used, jnp.abs(value), TINY), axis=1, keepdims=True)
    exponent = jnp.ceil(jnp.log(largest * (1.0 / STEPS)) * (1.0 / math.log(2.0)))
    code = jnp.clip(jnp.floor(value / step_size(exponent) + 0.5), -STEPS, STEPS)
    code = jnp.where(lane < used, code, jnp.where(lane == used, exponent, 0.0))
    partial[pl.ds(0, rows), :] = code.astype(jnp.int32).astype(jnp.int16)
    extra = partial.shape[0] - rows
    flags = dropped[...]
    if extra > flags.shape[0]:
        flags = jnp.concatenate([flags, jnp.zeros((extra - flags.shape[0], wide), F32)], axis=0)
    partial[pl.ds(rows, extra), :] = flags.astype(jnp.int32).astype(jnp.int16)


def step_size(exponent):
    return jnp.exp(exponent * math.log(2.0))


def tree_sum(values):
    while len(values) > 1:
        values = [a + b for a, b in zip(values[0::2], values[1::2])]
    return values[0]


def raise_kernel(side, used, groups, *refs):
    parts, (raised, stats) = refs[:-2], refs[-2:]
    rows, wide = raised.shape
    total = rows // side
    values, counts = [], []
    for part in parts:
        code = part[pl.ds(0, rows), :].astype(jnp.int32).astype(F32)
        values.append(code * step_size(code[:, used : used + 1]))
        counts.append(part[pl.ds(rows, part.shape[0] - rows), :].astype(jnp.int32))
    gone = PENALTY * tree_sum(counts).astype(F32)
    lines = [jnp.broadcast_to(gone[row : row + 1], (total // groups, wide)) for row in range(side * groups)]
    score = tree_sum(values) - jnp.concatenate(lines, axis=0)
    lane = lax.broadcasted_iota(jnp.int32, (rows, wide), 1)
    score = jnp.where(lane < used, score, NEG)
    peak = score[:total]
    for step in range(1, side):
        peak = jnp.maximum(peak, score[step * total : (step + 1) * total])
    peak = jnp.max(peak, axis=1, keepdims=True)
    added = jnp.zeros((total, wide), F32)
    for step in range(side):
        value = jnp.exp(score[step * total : (step + 1) * total] - peak)
        raised[pl.ds(step * total, total), :] = value
        added = added + value
    mass = jnp.sum(added, axis=1, keepdims=True)
    place = lax.broadcasted_iota(jnp.int32, stats.shape, 1)
    stats[...] = jnp.where(place == 0, peak, jnp.where(place == 1, mass, 0.0))


def sum_kernel(side, slots, pair, raised, own_stats, other_stats, rotated, cosine, sine, *rest):
    near, messages = rest[0], rest[1:]
    half = side // 2
    coef = cosine.shape[1]
    rows, wide = raised.shape
    total = rows // side
    owned = near.shape[0]
    orient = slots * owned
    peak, mass = own_stats[:, 0:1], own_stats[:, 1:2]
    if pair > 1:
        count = total // pair
        swapped = jnp.concatenate([other_stats[count:, :], other_stats[:count, :]], axis=0)
        top = jnp.maximum(peak, swapped[:, 0:1])
        factor = jnp.exp(peak - top)
        whole = mass * factor + swapped[:, 1:2] * jnp.exp(swapped[:, 0:1] - top)
        factor = factor / whole
    else:
        factor = 1.0 / mass
    posts = []
    columns = jnp.zeros((total, wide), F32)
    for step in range(side):
        prob = raised[pl.ds(step * total, total), :] * factor
        columns = columns + prob
        posts.append(prob.astype(BF16))
    post = jnp.concatenate(posts, axis=0)
    columns = jnp.sum(columns, axis=0, keepdims=True)
    column = lax.broadcasted_iota(jnp.int32, (orient, wide), 1)
    row = lax.broadcasted_iota(jnp.int32, (orient, wide), 0)
    same = (divided(column, orient)[1] == row) & (column < side * orient)
    masses = jnp.sum(jnp.where(same, columns, 0.0), axis=1, keepdims=True)
    spread = jnp.broadcast_to(masses, (orient, LANES))
    high = spread.astype(BF16)
    low = (spread - high.astype(F32)).astype(BF16)
    lane = lax.broadcasted_iota(jnp.int32, (orient, LANES), 1)
    tail = jnp.where(lane == 0, high.astype(F32), jnp.where(lane == 1, low.astype(F32), 0.0))
    near[:, pl.ds(2 * coef, LANES)] = spread[:owned]
    for slot in range(1, slots):
        piece = tail[slot * owned : (slot + 1) * owned]
        messages[slot - 1][:, pl.ds(2 * coef, LANES)] = piece.astype(BF16)

    post = jnp.transpose(post)
    for start in range(0, coef, LANES):
        lanes, far = pl.ds(start, LANES), pl.ds(coef + start, LANES)

        images = jnp.concatenate([rotated[:, lanes], rotated[:, far]], axis=1)
        moved = dot(post, images, ((1,), (0,)))

        def take(step, where):
            return moved[(step + half) * orient : (step + half + 1) * orient, where * LANES : (where + 1) * LANES]

        real, imag = take(0, 0), take(0, 1)
        for step in range(1, half + 1):
            c = cosine[half + step - 1 : half + step, lanes]
            s = sine[half + step - 1 : half + step, lanes]
            ra, rb = take(step, 0), take(-step, 0)
            ia, ib = take(step, 1), take(-step, 1)
            real = real + (ra + rb) * c - (ia - ib) * s
            imag = imag + (ia + ib) * c + (ra - rb) * s
        near[:, lanes] = real[:owned]
        near[:, far] = imag[:owned]
        for slot in range(1, slots):
            part = slice(slot * owned, (slot + 1) * owned)
            messages[slot - 1][:, lanes] = real[part].astype(BF16)
            messages[slot - 1][:, far] = imag[part].astype(BF16)


def finish_kernel(near, *rest):
    messages, (sums, mass) = rest[:-2], rest[-2:]
    owned, wide = sums.shape
    out = near[:, pl.ds(0, wide)]
    level = near[:, pl.ds(wide, LANES)][:, 0:1]
    for message in messages:
        out = out + message[:, pl.ds(0, wide)].astype(F32)
        tail = message[:, pl.ds(wide, LANES)].astype(F32)
        level = level + (tail[:, 0:1] + tail[:, 1:2])
    sums[...] = out
    row = lax.broadcasted_iota(jnp.int32, (owned, LANES), 0)
    lane = lax.broadcasted_iota(jnp.int32, (owned, LANES), 1)
    line = jnp.sum(jnp.where(row == lane, level, 0.0), axis=0, keepdims=True)
    mass[...] = line[:, :owned]


def call(kernel, outs, scratch=(), far=0):
    def size(value):
        return math.prod(value.shape) * jnp.dtype(value.dtype).itemsize

    def run(*args):
        held = [*args, *jax.tree.leaves(outs), *[value for value in scratch if value.memory_space == pltpu.MemorySpace.VMEM]]
        grant = 2 * sum(size(value) for value in held) + 4 * 1024 * 1024
        spaces = [pltpu.MemorySpace.HBM] * far + [pltpu.MemorySpace.VMEM] * (len(args) - far)
        return pl.pallas_call(
            kernel,
            in_specs=[pl.BlockSpec(memory_space=space) for space in spaces],
            out_shape=outs,
            scratch_shapes=list(scratch),
            compiler_params=pltpu.CompilerParams(vmem_limit_bytes=min(grant, 60 * 1024 * 1024)),
        )(*args)

    return run


def shaped(shape, dtype):
    return jax.ShapeDtypeStruct(shape, dtype)


def per_device(bands, places, images, references, noise_weight, masks):
    images, references, masks = images[0], references[0], masks[0]
    pair = 2 if places % 2 == 0 else 1
    slots = places // pair
    owned = references.shape[0]
    coef = noise_weight.shape[1]
    count = images.shape[0]
    side = math.isqrt(masks.shape[2])
    total = count * pair
    orient = slots * owned
    used = side * orient
    wide = round_up(used + 1, LANES)
    groups = pair * masks.shape[0]

    def across(value, axis, size, step):
        return lax.ppermute(value, axis, [(i, i ^ step) for i in range(size)])

    far_first = list(range(slots - 1, 0, -1))
    blocks = {}
    if pair > 1:
        other = across(images, "img", places, 1)
        other_masks = across(masks, "img", places, 1)
        blocks[0] = across(references, "img", places, 1)
    else:
        other, other_masks, blocks[0] = images, masks, references
    for slot in far_first:
        blocks[slot] = across(references, "img", places, slot * pair + pair - 1)

    def far_away(value):
        return pltpu.with_memory_space_constraint(value, pltpu.MemorySpace.HBM)

    def prepare(*refs):
        given, refs = refs[:3], refs[3:]
        prepare_kernel(side, pair, slots, owned, ("band", "img"), given, refs[0], refs[1], refs[2:7], refs[7:])

    rotated, cosine, sine, dropped, weight = call(
        prepare,
        (
            shaped((side * total, 2 * coef), BF16),
            shaped((8, coef), F32),
            shaped((8, coef), F32),
            shaped((side * groups, wide), F32),
            shaped(noise_weight.shape, noise_weight.dtype),
        ),
        (pltpu.VMEM(images.shape, images.dtype), pltpu.VMEM(masks.shape, masks.dtype), pltpu.SemaphoreType.DMA((3,))),
        3,
    )(*[far_away(value) for value in (images, masks, noise_weight)], other, other_masks)

    partial = call(
        functools.partial(score_kernel, side), shaped((side * total + round_up(side * groups, 16), wide), jnp.int16)
    )(weight, rotated, cosine, sine, dropped, *[blocks[slot] for slot in range(slots)])

    parts = {0: partial}
    for step in range(bands - 1, 0, -1):
        parts[step] = across(partial, "band", bands, step)
    raised, stats = call(
        functools.partial(raise_kernel, side, used, groups),
        (shaped((side * total, wide), F32), shaped((total, LANES), F32)),
    )(*[parts[step] for step in range(bands)])
    other_stats = across(stats, "img", places, 1) if pair > 1 else stats

    near, *messages = call(
        functools.partial(sum_kernel, side, slots, pair),
        (shaped((owned, 2 * coef + LANES), F32),) + (shaped((owned, 2 * coef + LANES), BF16),) * (slots - 1),
    )(raised, stats, other_stats, rotated, cosine, sine)
    arrived = {}
    for slot in far_first:
        arrived[slot] = across(messages[slot - 1], "img", places, slot * pair + pair - 1)
    if pair > 1:
        near = across(near, "img", places, 1)
    sums, mass = call(
        finish_kernel, (shaped((owned, 2 * coef), F32), shaped((1, owned), F32))
    )(near, *[arrived[slot] for slot in range(1, slots)])
    return sums[None], mass[0]


def solution(mesh):
    bands, places = mesh.shape["band"], mesh.shape["img"]
    in_specs = (
        P("band", "img", None),
        P("band", "img", None),
        P("band", None),
        P("band", "img", None, None),
    )
    out_specs = (P("band", "img", None), P("img"))

    def body(*args):
        return per_device(bands, places, *args)

    return jax.shard_map(body, mesh=mesh, in_specs=in_specs, out_specs=out_specs, check_vma=False)
```

```python
import functools
import math

import jax
import jax.numpy as jnp
from jax import lax
from jax.experimental import pallas as pl
from jax.experimental.pallas import tpu as pltpu
from jax.sharding import PartitionSpec as P


BOX = 256
PENALTY = 10000.0
LANES = 128
NEG = -3.0e38
TINY = 1.0e-30
STEPS = 32767.0


F32 = jnp.float32
BF16 = jnp.bfloat16


def round_up(value, step):
    return -(-value // step) * step


def divided(value, by):
    if by & (by - 1) == 0:
        return lax.shift_right_logical(value, jnp.int32(by.bit_length() - 1)), value & (by - 1)
    quotient = jnp.floor((value.astype(F32) + 0.5) * (1.0 / by)).astype(jnp.int32)
    return quotient, value - quotient * by


def dot(a, b, dims):
    return lax.dot_general(a, b, (dims, ((), ())), preferred_element_type=F32)


def prepare_kernel(side, pair, slots, owned, axes, given, other, other_mask, results, scratch):
    rotated, cosine, sine, dropped, own_weight = results
    own, own_mask, sems = scratch
    copies = []
    for number, (source, target) in enumerate(zip(given, (own, own_mask, own_weight))):
        copies.append(pltpu.make_async_copy(source, target, sems.at[number]))
        copies[-1].start()
    half = side // 2
    coef = cosine.shape[1]
    band = lax.axis_index(axes[0])
    place = lax.axis_index(axes[1])

    shape = (8, coef)
    row = lax.broadcasted_iota(jnp.int32, shape, 0)
    index = lax.broadcasted_iota(jnp.int32, shape, 1)

    freq_x = divided(index * 37 + band * 11, 257)[1] - 128
    freq_y = divided(index * 61 + band * 29, 129)[1]
    phase = jnp.where(row < half, (row + 1) * freq_x, (row - half + 1) * freq_y)
    phase = jnp.bitwise_and(phase + BOX // 2, BOX - 1) - BOX // 2
    angle = phase.astype(F32) * (2.0 * math.pi / BOX)
    cosine[...] = jnp.cos(angle)
    sine[...] = jnp.sin(angle)

    count = own.shape[0]
    total = pair * count
    for part, source in reversed(list(enumerate((own, other)[:pair]))):
        if part == 0:
            copies[0].wait()
        for start in range(0, coef, LANES):
            lanes, far = pl.ds(start, LANES), pl.ds(coef + start, LANES)

            def put(step, real, imag):
                rows = pl.ds((step + half) * total + part * count, count)
                rotated[rows, lanes] = real.astype(BF16)
                rotated[rows, far] = imag.astype(BF16)

            rotated[pl.ds(half * total + part * count, count), lanes] = source[:, lanes]
            rotated[pl.ds(half * total + part * count, count), far] = source[:, far]
            real = source[:, lanes].astype(F32)
            imag = source[:, far].astype(F32)
            for step in range(1, half + 1):
                c = cosine[step - 1 : step, lanes]
                s = sine[step - 1 : step, lanes]
                rc, rs, ic, iss = real * c, real * s, imag * c, imag * s
                put(step, rc - iss, rs + ic)
                put(-step, rc + iss, ic - rs)

    copies[1].wait()
    blocks, owners, shifts = own_mask.shape
    orient = slots * owned
    wide = dropped.shape[1]
    kept = own_mask[...].reshape(blocks * owners, shifts)
    if pair > 1:
        kept = jnp.concatenate([kept, other_mask[...].reshape(blocks * owners, shifts)], axis=0)
    gone = (1 - kept).astype(F32).astype(BF16)
    rows = kept.shape[0]

    def iota(shape, dim):
        return lax.broadcasted_iota(jnp.int32, shape, dim)

    step, column = divided(iota((1, side * wide), 1), wide)
    move_y, place_o = divided(column, orient)
    slot = divided(place_o, owned)[0]
    used = move_y < side
    wanted = jnp.where(used, step * side + move_y, -1)
    pick = (iota((shifts, side * wide), 0) == wanted).astype(F32).astype(BF16)
    owner = jnp.bitwise_xor(slot * pair + pair - 1, place)
    mine = divided(iota((rows, 1), 0), owners)[1] == owner
    groups = pair * blocks
    spread = iota((groups, 1), 0) == divided(iota((1, rows), 1), owners)[0]
    spread = spread.astype(F32).astype(BF16)
    chosen = jnp.where(mine, dot(gone, pick, ((1,), (0,))), 0.0).astype(BF16)
    level = dot(spread, chosen, ((1,), (0,)))
    dropped[...] = jnp.concatenate([level[:, step * wide : (step + 1) * wide] for step in range(side)], axis=0)
    copies[2].wait()


def score_kernel(side, weight, rotated, cosine, sine, dropped, *rest):
    blocks, partial = rest[:-1], rest[-1]
    half = side // 2
    coef = cosine.shape[1]
    orient = len(blocks) * blocks[0].shape[0]
    rows, wide = rotated.shape[0], partial.shape[1]
    norms = jnp.zeros((orient, LANES), F32)
    cross = jnp.zeros((rows, wide), F32)
    for start in range(0, coef, LANES):
        lanes, far = pl.ds(start, LANES), pl.ds(coef + start, LANES)
        scale = weight[:, lanes]
        real = jnp.concatenate([block[:, lanes].astype(F32) for block in blocks], axis=0)
        imag = jnp.concatenate([block[:, far].astype(F32) for block in blocks], axis=0)
        norms = norms + (real * real + imag * imag) * scale
        pieces = {0: ((real * scale).astype(BF16), (imag * scale).astype(BF16))}
        real, imag = pieces[0][0].astype(F32), pieces[0][1].astype(F32)
        for step in range(1, half + 1):
            c = cosine[half + step - 1 : half + step, lanes]
            s = sine[half + step - 1 : half + step, lanes]
            rc, rs, ic, iss = real * c, real * s, imag * c, imag * s
            pieces[step] = ((rc + iss).astype(BF16), (ic - rs).astype(BF16))
            pieces[-step] = ((rc - iss).astype(BF16), (ic + rs).astype(BF16))
        turned = [jnp.concatenate(pieces[step - half], axis=1) for step in range(side)]
        if wide > side * orient:
            turned.append(jnp.zeros((wide - side * orient, 2 * LANES), BF16))
        turned = jnp.concatenate(turned, axis=0)
        images = jnp.concatenate([rotated[:, lanes], rotated[:, far]], axis=1)
        cross = cross + dot(images, turned, ((1,), (1,)))
    norms = jnp.sum(norms, axis=1, keepdims=True)
    column = lax.broadcasted_iota(jnp.int32, (orient, wide), 1)
    row = lax.broadcasted_iota(jnp.int32, (orient, wide), 0)
    same = (divided(column, orient)[1] == row) & (column < side * orient)
    level = jnp.sum(jnp.where(same, norms, 0.0), axis=0, keepdims=True)
    value = cross - 0.5 * level
    used = side * orient
    lane = lax.broadcasted_iota(jnp.int32, (rows, wide), 1)
    largest = jnp.max(jnp.where(lane < used, jnp.abs(value), TINY), axis=1, keepdims=True)
    exponent = jnp.ceil(jnp.log(largest * (1.0 / STEPS)) * (1.0 / math.log(2.0)))
    code = jnp.clip(jnp.floor(value / step_size(exponent) + 0.5), -STEPS, STEPS)
    code = jnp.where(lane < used, code, jnp.where(lane == used, exponent, 0.0))
    partial[pl.ds(0, rows), :] = code.astype(jnp.int32).astype(jnp.int16)
    extra = partial.shape[0] - rows
    flags = dropped[...]
    if extra > flags.shape[0]:
        flags = jnp.concatenate([flags, jnp.zeros((extra - flags.shape[0], wide), F32)], axis=0)
    partial[pl.ds(rows, extra), :] = flags.astype(jnp.int32).astype(jnp.int16)


def step_size(exponent):
    return jnp.exp(exponent * math.log(2.0))


def tree_sum(values):
    while len(values) > 1:
        left = values[len(values) // 2 * 2 :]
        values = [a + b for a, b in zip(values[0::2], values[1::2])] + left
    return values[0]


def decode(part, rows, used):
    code = part[pl.ds(0, rows), :].astype(jnp.int32).astype(F32)
    value = code * step_size(code[:, used : used + 1])
    return value, part[pl.ds(rows, part.shape[0] - rows), :].astype(jnp.int32)


def decode_kernel(used, *refs):
    parts, (first, rest, counts) = refs[:-3], refs[-3:]
    decoded = [decode(part, first.shape[0], used) for part in parts]
    first[...] = decoded[0][0]
    rest[...] = tree_sum([value for value, _ in decoded[1:]])
    counts[...] = sum(count for _, count in decoded)


def raise_kernel(side, used, groups, last, first, rest, early, raised, stats):
    rows, wide = raised.shape
    total = rows // side
    value, count = decode(last, rows, used)
    gone = PENALTY * (early[...] + count).astype(F32)
    lines = [jnp.broadcast_to(gone[row : row + 1], (total // groups, wide)) for row in range(side * groups)]
    score = ((first[...] + value) + rest[...]) - jnp.concatenate(lines, axis=0)
    lane = lax.broadcasted_iota(jnp.int32, (rows, wide), 1)
    score = jnp.where(lane < used, score, NEG)
    peak = score[:total]
    for step in range(1, side):
        peak = jnp.maximum(peak, score[step * total : (step + 1) * total])
    peak = jnp.max(peak, axis=1, keepdims=True)
    added = jnp.zeros((total, wide), F32)
    for step in range(side):
        value = jnp.exp(score[step * total : (step + 1) * total] - peak)
        raised[pl.ds(step * total, total), :] = value
        added = added + value
    mass = jnp.sum(added, axis=1, keepdims=True)
    place = lax.broadcasted_iota(jnp.int32, stats.shape, 1)
    stats[...] = jnp.where(place == 0, peak, jnp.where(place == 1, mass, 0.0))


def sum_kernel(side, slots, pair, raised, own_stats, other_stats, rotated, cosine, sine, *rest):
    near, messages = rest[0], rest[1:]
    half = side // 2
    coef = cosine.shape[1]
    rows, wide = raised.shape
    total = rows // side
    owned = near.shape[0]
    orient = slots * owned
    peak, mass = own_stats[:, 0:1], own_stats[:, 1:2]
    if pair > 1:
        count = total // pair
        swapped = jnp.concatenate([other_stats[count:, :], other_stats[:count, :]], axis=0)
        top = jnp.maximum(peak, swapped[:, 0:1])
        factor = jnp.exp(peak - top)
        whole = mass * factor + swapped[:, 1:2] * jnp.exp(swapped[:, 0:1] - top)
        factor = factor / whole
    else:
        factor = 1.0 / mass
    posts = []
    columns = jnp.zeros((total, wide), F32)
    for step in range(side):
        prob = raised[pl.ds(step * total, total), :] * factor
        columns = columns + prob
        posts.append(prob.astype(BF16))
    post = jnp.concatenate(posts, axis=0)
    columns = jnp.sum(columns, axis=0, keepdims=True)
    column = lax.broadcasted_iota(jnp.int32, (orient, wide), 1)
    row = lax.broadcasted_iota(jnp.int32, (orient, wide), 0)
    same = (divided(column, orient)[1] == row) & (column < side * orient)
    masses = jnp.sum(jnp.where(same, columns, 0.0), axis=1, keepdims=True)
    spread = jnp.broadcast_to(masses, (orient, LANES))
    high = spread.astype(BF16)
    low = (spread - high.astype(F32)).astype(BF16)
    lane = lax.broadcasted_iota(jnp.int32, (orient, LANES), 1)
    tail = jnp.where(lane == 0, high.astype(F32), jnp.where(lane == 1, low.astype(F32), 0.0))
    near[:, pl.ds(2 * coef, LANES)] = spread[:owned]
    for slot in range(1, slots):
        piece = tail[slot * owned : (slot + 1) * owned]
        messages[slot - 1][:, pl.ds(2 * coef, LANES)] = piece.astype(BF16)

    post = jnp.transpose(post)
    for start in range(0, coef, LANES):
        lanes, far = pl.ds(start, LANES), pl.ds(coef + start, LANES)

        images = jnp.concatenate([rotated[:, lanes], rotated[:, far]], axis=1)
        moved = dot(post, images, ((1,), (0,)))

        def take(step, where):
            return moved[(step + half) * orient : (step + half + 1) * orient, where * LANES : (where + 1) * LANES]

        real, imag = take(0, 0), take(0, 1)
        for step in range(1, half + 1):
            c = cosine[half + step - 1 : half + step, lanes]
            s = sine[half + step - 1 : half + step, lanes]
            ra, rb = take(step, 0), take(-step, 0)
            ia, ib = take(step, 1), take(-step, 1)
            real = real + (ra + rb) * c - (ia - ib) * s
            imag = imag + (ia + ib) * c + (ra - rb) * s
        near[:, lanes] = real[:owned]
        near[:, far] = imag[:owned]
        for slot in range(1, slots):
            part = slice(slot * owned, (slot + 1) * owned)
            messages[slot - 1][:, lanes] = real[part].astype(BF16)
            messages[slot - 1][:, far] = imag[part].astype(BF16)


def finish_kernel(near, *rest):
    messages, (sums, mass) = rest[:-2], rest[-2:]
    owned, wide = sums.shape
    out = near[:, pl.ds(0, wide)]
    level = near[:, pl.ds(wide, LANES)][:, 0:1]
    for message in messages:
        out = out + message[:, pl.ds(0, wide)].astype(F32)
        tail = message[:, pl.ds(wide, LANES)].astype(F32)
        level = level + (tail[:, 0:1] + tail[:, 1:2])
    sums[...] = out
    row = lax.broadcasted_iota(jnp.int32, (owned, LANES), 0)
    lane = lax.broadcasted_iota(jnp.int32, (owned, LANES), 1)
    line = jnp.sum(jnp.where(row == lane, level, 0.0), axis=0, keepdims=True)
    mass[...] = line[:, :owned]


def call(kernel, outs, scratch=(), far=0):
    def size(value):
        return math.prod(value.shape) * jnp.dtype(value.dtype).itemsize

    def run(*args):
        held = [*args, *jax.tree.leaves(outs), *[value for value in scratch if value.memory_space == pltpu.MemorySpace.VMEM]]
        grant = 2 * sum(size(value) for value in held) + 4 * 1024 * 1024
        spaces = [pltpu.MemorySpace.HBM] * far + [pltpu.MemorySpace.VMEM] * (len(args) - far)
        return pl.pallas_call(
            kernel,
            in_specs=[pl.BlockSpec(memory_space=space) for space in spaces],
            out_shape=outs,
            scratch_shapes=list(scratch),
            compiler_params=pltpu.CompilerParams(vmem_limit_bytes=min(grant, 60 * 1024 * 1024)),
        )(*args)

    return run


def shaped(shape, dtype):
    return jax.ShapeDtypeStruct(shape, dtype)


def per_device(bands, places, images, references, noise_weight, masks):
    images, references, masks = images[0], references[0], masks[0]
    pair = 2 if places % 2 == 0 else 1
    slots = places // pair
    owned = references.shape[0]
    coef = noise_weight.shape[1]
    count = images.shape[0]
    side = math.isqrt(masks.shape[2])
    total = count * pair
    orient = slots * owned
    used = side * orient
    wide = round_up(used + 1, LANES)
    groups = pair * masks.shape[0]

    def across(value, axis, size, step):
        return lax.ppermute(value, axis, [(i, i ^ step) for i in range(size)])

    far_first = list(range(slots - 1, 0, -1))
    blocks = {}
    if pair > 1:
        other = across(images, "img", places, 1)
        other_masks = across(masks, "img", places, 1)
        blocks[0] = across(references, "img", places, 1)
    else:
        other, other_masks, blocks[0] = images, masks, references
    for slot in far_first:
        blocks[slot] = across(references, "img", places, slot * pair + pair - 1)

    def far_away(value):
        return pltpu.with_memory_space_constraint(value, pltpu.MemorySpace.HBM)

    def prepare(*refs):
        given, refs = refs[:3], refs[3:]
        prepare_kernel(side, pair, slots, owned, ("band", "img"), given, refs[0], refs[1], refs[2:7], refs[7:])

    rotated, cosine, sine, dropped, weight = call(
        prepare,
        (
            shaped((side * total, 2 * coef), BF16),
            shaped((8, coef), F32),
            shaped((8, coef), F32),
            shaped((side * groups, wide), F32),
            shaped(noise_weight.shape, noise_weight.dtype),
        ),
        (pltpu.VMEM(images.shape, images.dtype), pltpu.VMEM(masks.shape, masks.dtype), pltpu.SemaphoreType.DMA((3,))),
        3,
    )(*[far_away(value) for value in (images, masks, noise_weight)], other, other_masks)

    partial = call(
        functools.partial(score_kernel, side), shaped((side * total + round_up(side * groups, 16), wide), jnp.int16)
    )(weight, rotated, cosine, sine, dropped, *[blocks[slot] for slot in range(slots)])

    parts = {0: partial}
    for step in range(bands - 1, 0, -1):
        parts[step] = across(partial, "band", bands, step)
    plane = shaped((side * total, wide), F32)
    flags = partial.shape[0] - side * total
    early = call(
        functools.partial(decode_kernel, used), (plane, plane, shaped((flags, wide), jnp.int32))
    )(*[parts[step] for step in range(bands) if step != 1])
    raised, stats = call(
        functools.partial(raise_kernel, side, used, groups), (plane, shaped((total, LANES), F32))
    )(parts[1], *early)
    other_stats = across(stats, "img", places, 1) if pair > 1 else stats

    near, *messages = call(
        functools.partial(sum_kernel, side, slots, pair),
        (shaped((owned, 2 * coef + LANES), F32),) + (shaped((owned, 2 * coef + LANES), BF16),) * (slots - 1),
    )(raised, stats, other_stats, rotated, cosine, sine)
    arrived = {}
    for slot in far_first:
        arrived[slot] = across(messages[slot - 1], "img", places, slot * pair + pair - 1)
    if pair > 1:
        near = across(near, "img", places, 1)
    sums, mass = call(
        finish_kernel, (shaped((owned, 2 * coef), F32), shaped((1, owned), F32))
    )(near, *[arrived[slot] for slot in range(1, slots)])
    return sums[None], mass[0]


def solution(mesh):
    bands, places = mesh.shape["band"], mesh.shape["img"]
    in_specs = (
        P("band", "img", None),
        P("band", "img", None),
        P("band", None),
        P("band", "img", None, None),
    )
    out_specs = (P("band", "img", None), P("img"))

    def body(*args):
        return per_device(bands, places, *args)

    return jax.shard_map(body, mesh=mesh, in_specs=in_specs, out_specs=out_specs, check_vma=False)
```
